512 devices in a mesh: xi: 32 (over x, z), eta: 16 (over y, core).
Axes of the slice: x: 4, y: 8, z: 8, core: 2. Of those that a mesh axis runs over, the one named last changes fastest.
Arguments:
- residual: float32 [5, 2048, 2048], P(None, 'xi', 'eta'), may hold values from -30 to 30
- left_eta: float32 [5, 5, 2048, 2048], P(None, None, 'xi', 'eta'), may hold values from -2.7 to 2.7
- middle: float32 [5, 5, 2048, 2048], P(None, None, 'xi', 'eta'), may hold values from -2.7 to 2.7
- right_xi: float32 [5, 5, 2048, 2048], P(None, None, 'xi', 'eta'), may hold values from -2.7 to 2.7
- speed_eta: float32 [5, 2048, 2048], P(None, 'xi', 'eta'), may hold values from -120.25 to 120.25
- speed_xi: float32 [5, 2048, 2048], P(None, 'xi', 'eta'), may hold values from -120.25 to 120.25
- damping_eta: float32 [2048, 2048], P('xi', 'eta'), may hold values from 0.5 to 3
- damping_xi: float32 [2048, 2048], P('xi', 'eta'), may hold values from 0.5 to 3
Outputs:
- increment: float32 [5, 2048, 2048], P(None, 'xi', 'eta')
The draws below stay inside these ranges and needn't reach their ends.
All inputs are finite; a program needn't handle non-finite values.
Results may differ from the reference program's by a relative error of at most 0.000041.
Values sent between devices are 32-bit elements; how exact they have to be, the bound alone decides.
No kernel may reach another device: no remote copies, remote signals or barrier semaphores. Data moves between devices by JAX's collectives and lax.ppermute only.
A program may use at most 128 MiB of HBM per device.

```python
import math
import jax
import jax.numpy as jnp
from jax import lax

SPAN = 2
FIELDS = 5
NXI = 2048
NETA = 1024


def speeds_common(key, base_shape, full_shape):
    key_scale, key_sign, key_noise = jax.random.split(key, 3)
    magnitude = jnp.exp(jax.random.uniform(key_scale, base_shape, jnp.float32, math.log(20.0), math.log(120.0)))
    heading = 2.0 * jax.random.bernoulli(key_sign, 0.5, base_shape).astype(jnp.float32) - 1.0
    jitter = jax.random.uniform(key_noise, full_shape, jnp.float32, -0.25, 0.25)
    return heading * magnitude + jitter


def draw_speed_eta(key, part):
    values = speeds_common(jax.random.fold_in(key, 11), (FIELDS, NXI, 1, SPAN), (FIELDS, NXI, NETA, SPAN))
    return values.reshape(FIELDS, NXI, NETA * SPAN)


def draw_speed_xi(key, part):
    return speeds_common(jax.random.fold_in(key, 23), (FIELDS, 1, NETA * SPAN), (FIELDS, NXI, NETA * SPAN))


def levels(own_key, shape, shards, least, high):
    factor_of, own = 1.0, jax.random.fold_in(own_key, 6)
    for position, parts in shards:
        steps = jnp.exp(jax.random.uniform(jax.random.fold_in(own, position), (parts,), jnp.float32, least / len(shards), high / len(shards)))
        factor_of = factor_of * jnp.repeat(steps, shape[position] // parts).reshape([-1 if axis == position else 1 for axis in range(len(shape))])
    return factor_of


def noise(own_key, dims, scale, reach, cuts=(), held_as=jnp.bfloat16):
    loudness = levels(own_key, dims, cuts, -0.22, 0.18) if cuts else 1.0
    values = jax.random.normal(own_key, dims, jnp.float32) * scale * loudness
    return jnp.minimum(jnp.maximum(values, -reach), reach).astype(held_as)


def setup_inputs(seed: int = 0) -> dict:
    key_list = jax.random.split(jax.random.key(seed), 9)
    return {
        "residual": noise(key_list[0], (FIELDS, NXI, NETA * SPAN), 5.0, 30.0, ((1, 32), (2, 16)), jnp.float32),
        "left_eta": noise(key_list[1], (FIELDS, FIELDS, NXI, NETA * SPAN), 0.45, 2.7, ((2, 32), (3, 16)), jnp.float32),
        "middle": noise(key_list[2], (FIELDS, FIELDS, NXI, NETA * SPAN), 0.45, 2.7, ((2, 32), (3, 16)), jnp.float32),
        "right_xi": noise(key_list[3], (FIELDS, FIELDS, NXI, NETA * SPAN), 0.45, 2.7, ((2, 32), (3, 16)), jnp.float32),
        "speed_eta": draw_speed_eta(jax.random.fold_in(key_list[8], 71), 0),
        "speed_xi": draw_speed_xi(jax.random.fold_in(key_list[8], 71), 0),
        "damping_eta": jnp.clip(jnp.exp(math.log(3.0) - 1.7917595 * jax.random.uniform(key_list[6], (NXI, NETA * SPAN), jnp.float32) ** levels(key_list[6], (NXI, NETA * SPAN), ((0, 32), (1, 16)), -0.2, 0.2)), 0.5, 3.0),
        "damping_xi": jnp.clip(jnp.exp(math.log(3.0) - 1.7917595 * jax.random.uniform(key_list[7], (NXI, NETA * SPAN), jnp.float32) ** levels(key_list[7], (NXI, NETA * SPAN), ((0, 32), (1, 16)), -0.2, 0.2)), 0.5, 3.0),
    }


def apply_cells(matrix, values):
    return jnp.sum(matrix * values[None], axis=1)


def penta_rows(speed_ext, damp_ext):
    damp_low = damp_ext[:-2]
    damp_mid = damp_ext[1:-1]
    damp_high = damp_ext[2:]
    inner_low = -0.5 * speed_ext[:-2] - 2.0 * damp_low - 2.0 * damp_mid
    inner_up = 0.5 * speed_ext[2:] - 2.0 * damp_mid - 2.0 * damp_high
    middle = jnp.broadcast_to(1.0 + damp_low + 4.0 * damp_mid + damp_high, inner_low.shape)
    outer_low = jnp.broadcast_to(damp_low, inner_low.shape)
    outer_up = jnp.broadcast_to(damp_high, inner_low.shape)
    return (outer_low, inner_low, middle, inner_up, outer_up)


def band_solve(coeffs, values):
    outer_low, inner_low, middle, inner_up, outer_up = coeffs
    flat_zero = jnp.zeros(middle.shape[1:], jnp.float32)
    value_zero = jnp.zeros(values.shape[1:], jnp.float32)

    def forward(state, incoming):
        next_one, skip_one, known_one, next_two, skip_two, known_two = state
        far_low, near_low, centre, near_up, far_up, source = incoming
        reduced_low = near_low - far_low * next_two
        pivot_value = centre - far_low * skip_two - reduced_low * next_one
        next_new = (near_up - reduced_low * skip_one) / pivot_value
        skip_new = far_up / pivot_value
        known_new = (source - far_low[None] * known_two - reduced_low[None] * known_one) / pivot_value[None]
        return (next_new, skip_new, known_new, next_one, skip_one, known_one), (next_new, skip_new, known_new)

    initial = (flat_zero, flat_zero, value_zero, flat_zero, flat_zero, value_zero)
    unused_state, factors = lax.scan(forward, initial, (outer_low, inner_low, middle, inner_up, outer_up, values))

    def backward(state, incoming):
        later_one, later_two = state
        next_factor, skip_factor, known_part = incoming
        result = known_part - next_factor[None] * later_one - skip_factor[None] * later_two
        return (result, later_one), result

    unused_back, solved = lax.scan(backward, (value_zero, value_zero), factors, reverse=True)
    return solved


def periodic_solve(coeffs, values):
    outer_low, inner_low, middle, inner_up, outer_up = coeffs
    line_size = middle.shape[0]
    head = tuple(band_part[:line_size - 2] for band_part in coeffs)
    blanks = jnp.zeros_like(values[:line_size - 2])
    column_a = blanks.at[0].set(outer_low[0]).at[line_size - 4].set(outer_up[line_size - 4]).at[line_size - 3].set(inner_up[line_size - 3])
    column_b = blanks.at[0].set(inner_low[0]).at[1].set(outer_low[1]).at[line_size - 3].set(outer_up[line_size - 3])
    solved = band_solve(head, jnp.stack([values[:line_size - 2], column_a, column_b], axis=1))
    base_part = solved[:, 0]
    resp_a = solved[:, 1]
    resp_b = solved[:, 2]
    row_a = line_size - 2
    row_b = line_size - 1
    entry_aa = middle[row_a] - outer_low[row_a] * resp_a[row_a - 2] - inner_low[row_a] * resp_a[row_a - 1] - outer_up[row_a] * resp_a[0]
    entry_ab = inner_up[row_a] - outer_low[row_a] * resp_b[row_a - 2] - inner_low[row_a] * resp_b[row_a - 1] - outer_up[row_a] * resp_b[0]
    source_a = values[row_a] - outer_low[row_a] * base_part[row_a - 2] - inner_low[row_a] * base_part[row_a - 1] - outer_up[row_a] * base_part[0]
    entry_ba = inner_low[row_b] - outer_low[row_b] * resp_a[row_b - 2] - inner_up[row_b] * resp_a[0] - outer_up[row_b] * resp_a[1]
    entry_bb = middle[row_b] - outer_low[row_b] * resp_b[row_b - 2] - inner_up[row_b] * resp_b[0] - outer_up[row_b] * resp_b[1]
    source_b = values[row_b] - outer_low[row_b] * base_part[row_b - 2] - inner_up[row_b] * base_part[0] - outer_up[row_b] * base_part[1]
    determinant = entry_aa * entry_bb - entry_ab * entry_ba
    value_a = (source_a * entry_bb - entry_ab * source_b) / determinant
    value_b = (entry_aa * source_b - entry_ba * source_a) / determinant
    remaining = base_part - resp_a * value_a[None] - resp_b * value_b[None]
    return jnp.concatenate([remaining, value_a[None], value_b[None]], axis=0)


def reference(residual, left_eta, middle, right_xi, speed_eta, speed_xi, damping_eta, damping_xi):
    first_pass = apply_cells(left_eta, residual)
    line_data = jnp.moveaxis(first_pass.reshape(FIELDS, NXI, NETA, SPAN), 2, 0)
    speeds = jnp.moveaxis(speed_eta.reshape(FIELDS, NXI, NETA, SPAN), 2, 0)
    damps = jnp.moveaxis(damping_eta.reshape(1, NXI, NETA, SPAN), 2, 0)
    padding = ((1, 1), (0, 0), (0, 0), (0, 0))
    coeffs = penta_rows(jnp.pad(speeds, padding), jnp.pad(damps, padding))
    solved = band_solve(coeffs, line_data[:, None])[:, 0]
    eta_sol = jnp.moveaxis(solved, 0, 2).reshape(FIELDS, NXI, NETA * SPAN)
    mixed = apply_cells(middle, eta_sol)
    line_data = jnp.moveaxis(mixed, 1, 0)
    speeds = jnp.moveaxis(speed_xi, 1, 0)
    damps = damping_xi[:, None]
    speed_ext = jnp.concatenate([speeds[-1:], speeds, speeds[:1]], axis=0)
    damp_ext = jnp.concatenate([damps[-1:], damps, damps[:1]], axis=0)
    coeffs = penta_rows(speed_ext, damp_ext)
    xi_sol = jnp.moveaxis(periodic_solve(coeffs, line_data), 0, 1)
    return apply_cells(right_xi, xi_sol)
```

```python
import functools

import jax
import jax.numpy as jnp
from jax import lax
from jax.experimental import pallas as pl
from jax.experimental.pallas import tpu as pltpu
from jax.sharding import PartitionSpec as P

SPAN = 2
FIELDS = 5
STEPS = 8
LANES = 128
FORM = 20
SENT = 24


def merge(low, high):
    a_p0, a_p1, a_q0, a_q1 = (low[5 * x : 5 * x + 5] for x in range(4))
    b_p0, b_p1, b_q0, b_q1 = (high[5 * x : 5 * x + 5] for x in range(4))
    l00, l01, l10, l11 = b_p0[1], b_p0[2], b_p1[1], b_p1[2]
    u00, u01, u10, u11 = a_q0[3], a_q0[4], a_q1[3], a_q1[4]
    m00 = 1.0 - l00 * u00 - l01 * u10
    m01 = -(l00 * u01 + l01 * u11)
    m10 = -(l10 * u00 + l11 * u10)
    m11 = 1.0 - l10 * u01 - l11 * u11
    inv = 1.0 / (m00 * m11 - m01 * m10)
    m00, m01, m10, m11 = m00 * inv, m01 * inv, m10 * inv, m11 * inv
    r0 = [b_p0[0] - l00 * a_q0[0] - l01 * a_q1[0]]
    r1 = [b_p1[0] - l10 * a_q0[0] - l11 * a_q1[0]]
    for c in (1, 2):
        r0.append(-(l00 * a_q0[c] + l01 * a_q1[c]))
        r1.append(-(l10 * a_q0[c] + l11 * a_q1[c]))
    r0 += [b_p0[3], b_p0[4]]
    r1 += [b_p1[3], b_p1[4]]
    p0 = [m11 * s - m01 * t for s, t in zip(r0, r1)]
    p1 = [m00 * t - m10 * s for s, t in zip(r0, r1)]

    def through_p(row):
        out = [row[c] - row[3] * p0[c] - row[4] * p1[c] for c in (0, 1, 2)]
        return out + [-(row[3] * p0[c] + row[4] * p1[c]) for c in (3, 4)]

    q0, q1 = through_p(a_q0), through_p(a_q1)

    def through_q(row):
        out = [row[0] - row[1] * q0[0] - row[2] * q1[0]]
        out += [-(row[1] * q0[c] + row[2] * q1[c]) for c in (1, 2)]
        return out + [row[c] - row[1] * q0[c] - row[2] * q1[c] for c in (3, 4)]

    joined = through_p(a_p0) + through_p(a_p1) + through_q(b_q0) + through_q(b_q1)
    return joined, p0 + p1 + q0 + q1


def value_of(row, outside):
    return (row[0] - row[1] * outside[0] - row[2] * outside[1]) - (
        row[3] * outside[2] + row[4] * outside[3]
    )


def plain_form(form, damp_low, speed_low, damp_high, speed_high):
    turn_low = 2.0 * damp_low + 0.5 * speed_low
    turn_high = 0.5 * speed_high - 2.0 * damp_high
    rows = []
    for x in range(4):
        k, a, b, c, d = form[5 * x : 5 * x + 5]
        rows.append([k, a * damp_low, b - a * turn_low, c + d * turn_high, d * damp_high])
    first, last = rows[0], rows[3]
    e00, e01 = 1.0 + first[1], first[4]
    e10, e11 = last[1], 1.0 + last[4]
    inv = 1.0 / (e00 * e11 - e01 * e10)
    e00, e01, e10, e11 = e00 * inv, e01 * inv, e10 * inv, e11 * inv
    new_first = [e11 * s - e01 * t for s, t in zip(first, last)]
    new_last = [e00 * t - e10 * s for s, t in zip(first, last)]
    inner = [
        [row[c] - row[1] * new_first[c] - row[4] * new_last[c] for c in range(5)]
        for row in rows[1:3]
    ]
    return new_first + inner[0] + inner[1] + new_last


def rim_terms(outside, first, last, damp_low, speed_low, damp_high, speed_high):
    l0, l1, r0, r1 = outside
    low = damp_low * (l0 - 2.0 * l1 + first) - 0.5 * speed_low * l1
    high = damp_high * (last - 2.0 * r0 + r1) + 0.5 * speed_high * r0
    return [low, l1, r0, high]


def section_rows():
    return lax.broadcasted_iota(jnp.int32, (STEPS, LANES), 0)


def reduce_sections(values, speeds, damps, cols_ref, form_ref):
    row = section_rows()
    zero = jnp.zeros((STEPS, LANES), jnp.float32)

    def below(x):
        return jnp.where(row == 0, zero, pltpu.roll(x, 1, 0))

    def above(x):
        return jnp.where(row == STEPS - 1, zero, pltpu.roll(x, STEPS - 1, 0))

    damp = [damps(j) for j in range(STEPS)]
    damp = [below(damp[-1])] + damp + [above(damp[0])]
    edge = [2.0 * (damp[j] + damp[j + 1]) for j in range(STEPS + 1)]
    centre = [1.0 + damp[j] + 4.0 * damp[j + 1] + damp[j + 2] for j in range(STEPS)]
    far_first = jnp.where(row == 0, 1.0, damp[0])
    far_last = jnp.where(row == STEPS - 1, 1.0, damp[STEPS + 1])
    for f in range(FIELDS):
        half = [0.5 * speeds(f, j) for j in range(STEPS)]
        half = [below(half[-1])] + half + [above(half[0])]
        parts = []
        for j in range(STEPS):
            far_low = damp[j]
            near_low = -(half[j] + edge[j])
            near_up = half[j + 2] - edge[j + 1]
            far_up = far_last if j == STEPS - 1 else damp[j + 2]
            source = values(f, j)
            if j == 0:
                inv = 1.0 / centre[0]
                parts.append(
                    [source * inv, far_first * inv, near_low * inv, near_up * inv, far_up * inv]
                )
                continue
            k1, a1, b1, n1, m1 = parts[j - 1]
            if j == 1:
                inv = 1.0 / (centre[1] - near_low * n1)
                parts.append(
                    [
                        (source - near_low * k1) * inv,
                        -(near_low * a1) * inv,
                        (far_low - near_low * b1) * inv,
                        (near_up - near_low * m1) * inv,
                        far_up * inv,
                    ]
                )
                continue
            k2, a2, b2, n2, m2 = parts[j - 2]
            lead = near_low - far_low * n2
            inv = 1.0 / ((centre[j] - far_low * m2) - lead * n1)
            parts.append(
                [
                    ((source - far_low * k2) - lead * k1) * inv,
                    -(far_low * a2 + lead * a1) * inv,
                    -(far_low * b2 + lead * b1) * inv,
                    (near_up - lead * m1) * inv,
                    far_up * inv,
                ]
            )
        cols = [None] * STEPS
        cols[7] = parts[7]
        k, a, b, n, m = parts[6]
        nxt = cols[7]
        cols[6] = [
            k - n * nxt[0],
            a - n * nxt[1],
            b - n * nxt[2],
            m - n * nxt[3],
            -(n * nxt[4]),
        ]
        for j in range(STEPS - 3, -1, -1):
            k, a, b, n, m = parts[j]
            nxt, aft = cols[j + 1], cols[j + 2]
            cols[j] = [
                k - n * nxt[0] - m * aft[0],
                a - n * nxt[1] - m * aft[1],
                b - n * nxt[2] - m * aft[2],
                -(n * nxt[3] + m * aft[3]),
                -(n * nxt[4] + m * aft[4]),
            ]
        for j in range(STEPS):
            for c in range(5):
                cols_ref[c, f, j] = cols[j][c]
        for x, j in enumerate((0, 1, STEPS - 2, STEPS - 1)):
            for c in range(5):
                form_ref[5 * x + c, pl.ds(STEPS * f, STEPS), :] = cols[j][c]


def merge_rows(src_ref, count, meet_ref):
    low = [src_ref[v, pl.ds(0, count, stride=2), :] for v in range(FORM)]
    high = [src_ref[v, pl.ds(1, count, stride=2), :] for v in range(FORM)]
    joined, meet = merge(low, high)
    for v in range(FORM):
        meet_ref[v] = meet[v]
    return joined


def merge_tree(form_ref, mid_ref, small_ref, meets):
    for v, item in enumerate(merge_rows(form_ref, 20, meets[0])):
        mid_ref[v] = item
    for v, item in enumerate(merge_rows(mid_ref, 10, meets[1])):
        small_ref[v] = item
    return merge_rows(small_ref, 5, meets[2])


def spread_tree(outside, meets, spreads):
    for meet_ref, out_ref, count in zip(meets[::-1], spreads, (5, 10, 20)):
        p0, p1, q0, q1 = (
            value_of([meet_ref[5 * x + c] for c in range(5)], outside) for x in range(4)
        )
        even = (outside[0], outside[1], p0, p1)
        odd = (q0, q1, outside[2], outside[3])
        for x in range(4):
            out_ref[x, pl.ds(0, count, stride=2), :] = even[x]
            out_ref[x, pl.ds(1, count, stride=2), :] = odd[x]
        outside = [out_ref[x] for x in range(4)]


def section_values(cols_ref, spread_ref, f, j):
    outside = [spread_ref[x, pl.ds(STEPS * f, STEPS), :] for x in range(4)]
    return value_of([cols_ref[c, f, j] for c in range(5)], outside)


def apply_cells(matrix_ref, values, out_ref):
    for f in range(FIELDS):
        total = matrix_ref[f, 0] * values[0]
        for g in range(1, FIELDS):
            total = total + matrix_ref[f, g] * values[g]
        out_ref[f] = total


def rim_rows(first, last):
    return [first[0], first[1], last[0], last[1]]


def to_eta_rows(block):
    beside = pltpu.roll(block, LANES - 1, 1)
    return jnp.transpose(jnp.concatenate([block, beside], axis=0))


def from_eta_rows(rows):
    both = jnp.transpose(rows)
    half = both.shape[0] // 2
    lane = lax.broadcasted_iota(jnp.int32, (half, LANES), 1)
    return jnp.where(lane % 2 == 0, both[:half], pltpu.roll(both[half:], 1, 1))


def eta_reduce_kernel(
    residual_ref, left_ref, speed_ref, damp_ref,
    send_ref, cols_ref, meet0_ref, meet1_ref, meet2_ref,
    work_ref, turned_ref, form_ref, mid_ref, small_ref,
):
    apply_cells(left_ref, [residual_ref[g] for g in range(FIELDS)], work_ref)
    for f in range(FIELDS):
        turned_ref[f] = to_eta_rows(work_ref[f])
        turned_ref[FIELDS + f] = to_eta_rows(speed_ref[f])
    turned_ref[2 * FIELDS] = to_eta_rows(damp_ref[...])

    def cell(index, j):
        return turned_ref[index, pl.ds(SPAN * j, STEPS, stride=SPAN * STEPS), :]

    reduce_sections(
        cell,
        lambda f, j: cell(FIELDS + f, j),
        lambda j: cell(2 * FIELDS, j),
        cols_ref,
        form_ref,
    )
    block = merge_tree(form_ref, mid_ref, small_ref, (meet0_ref, meet1_ref, meet2_ref))
    for v in range(FORM):
        send_ref[pl.ds(FIELDS * v, FIELDS), :] = block[v]
    final = SPAN * (STEPS * STEPS - 1)
    for f in range(FIELDS):
        rims = (
            turned_ref[2 * FIELDS, pl.ds(0, 1), :],
            turned_ref[FIELDS + f, pl.ds(0, 1), :],
            turned_ref[2 * FIELDS, pl.ds(final, 1), :],
            turned_ref[FIELDS + f, pl.ds(final, 1), :],
        )
        for r in range(4):
            send_ref[pl.ds(FIELDS * (FORM + r) + f, 1), :] = rims[r]


def eta_outside(place_ref, got_ref, form_ref, mid_ref, small_ref, meets, spreads, all_ref, own_ref):
    row = section_rows()
    zero = jnp.zeros((STEPS, LANES), jnp.float32)
    rows_each = SENT * FIELDS
    pair_forms, pair_meets, rims = [], [], []
    for f in range(FIELDS):
        halves = [
            [
                got_ref[pl.ds(rows_each * side + FIELDS * v + f, STEPS, stride=2 * rows_each), :]
                for v in range(SENT)
            ]
            for side in range(2)
        ]
        even, odd = halves
        rim_even = (
            jnp.where(row == 0, zero, pltpu.roll(odd[22], 1, 0)),
            jnp.where(row == 0, zero, pltpu.roll(odd[23], 1, 0)),
            odd[20],
            odd[21],
        )
        rim_odd = (
            even[22],
            even[23],
            jnp.where(row == STEPS - 1, zero, pltpu.roll(even[20], STEPS - 1, 0)),
            jnp.where(row == STEPS - 1, zero, pltpu.roll(even[21], STEPS - 1, 0)),
        )
        low = plain_form(even[:FORM], *rim_even)
        high = plain_form(odd[:FORM], *rim_odd)
        joined, meet = merge(low, high)
        for v in range(FORM):
            form_ref[v, pl.ds(STEPS * f, STEPS), :] = joined[v]
        pair_meets.append(meet)
        pair_forms.append((low[:5], low[15:], high[:5], high[15:]))
        rims.append((rim_even, rim_odd))
    merge_tree(form_ref, mid_ref, small_ref, meets)
    nothing = jnp.zeros((FIELDS, LANES), jnp.float32)
    spread_tree([nothing] * 4, meets, spreads)
    place = place_ref[0]
    for f in range(FIELDS):
        l0, l1, r0, r1 = (spreads[2][x, pl.ds(STEPS * f, STEPS), :] for x in range(4))
        p0, p1, q0, q1 = (
            value_of(pair_meets[f][5 * x : 5 * x + 5], (l0, l1, r0, r1)) for x in range(4)
        )
        for side, around in enumerate(((l0, l1, p0, p1), (q0, q1, r0, r1))):
            first = value_of(pair_forms[f][2 * side], around)
            last = value_of(pair_forms[f][2 * side + 1], around)
            for x, item in enumerate(rim_terms(around, first, last, *rims[f][side])):
                all_ref[x, side, pl.ds(STEPS * f, STEPS), :] = item
        side = lax.rem(place, 2)
        pair = lax.div(place, 2)
        for x in range(4):
            own_ref[x, pl.ds(f, 1), :] = all_ref[x, side, pl.ds(STEPS * f + pair, 1), :]


def eta_finish_kernel(
    place_ref, got_ref, eta_cols_ref, eta_meet0_ref, eta_meet1_ref, eta_meet2_ref,
    middle_ref, speed_ref, damp_ref,
    send_ref, cols_ref, meet0_ref, meet1_ref, meet2_ref,
    form_ref, mid_ref, small_ref, spread0_ref, spread1_ref, spread2_ref, all_ref, own_ref,
    turned_ref, mixed_ref, square_ref,
):
    spreads = (spread0_ref, spread1_ref, spread2_ref)
    meets = (meet0_ref, meet1_ref, meet2_ref)
    eta_outside(place_ref, got_ref, form_ref, mid_ref, small_ref, meets, spreads, all_ref, own_ref)
    spread_tree(
        [own_ref[x] for x in range(4)], (eta_meet0_ref, eta_meet1_ref, eta_meet2_ref), spreads
    )
    solved = []
    for f in range(FIELDS):
        for j in range(STEPS):
            turned_ref[f, pl.ds(SPAN * j, STEPS, stride=SPAN * STEPS), :] = section_values(
                eta_cols_ref, spread2_ref, f, j
            )
        solved.append(from_eta_rows(turned_ref[f]))
    apply_cells(middle_ref, solved, mixed_ref)
    reduce_sections(
        lambda f, j: mixed_ref[f, pl.ds(j, STEPS, stride=STEPS), :],
        lambda f, j: speed_ref[f, pl.ds(j, STEPS, stride=STEPS), :],
        lambda j: damp_ref[pl.ds(j, STEPS, stride=STEPS), :],
        cols_ref,
        form_ref,
    )
    block = merge_tree(form_ref, mid_ref, small_ref, meets)
    for v in range(FORM):
        square_ref[pl.ds(FIELDS * v, FIELDS), :] = block[v]
    final = STEPS * STEPS - 1
    for f in range(FIELDS):
        rims = (
            damp_ref[pl.ds(0, 1), :],
            speed_ref[f, pl.ds(0, 1), :],
            damp_ref[pl.ds(final, 1), :],
            speed_ref[f, pl.ds(final, 1), :],
        )
        for r in range(4):
            square_ref[pl.ds(FIELDS * (FORM + r) + f, 1), :] = rims[r]
    square_ref[pl.ds(SENT * FIELDS, LANES - SENT * FIELDS), :] = jnp.zeros(
        (LANES - SENT * FIELDS, LANES), jnp.float32
    )
    send_ref[...] = jnp.transpose(square_ref[...])


def xi_loop_kernel(got_ref, send_ref, square_ref):
    square_ref[...] = jnp.transpose(got_ref[...])
    items = [square_ref[pl.ds(FIELDS * v, FIELDS), :] for v in range(SENT)]
    width = 4

    def from_below(x, distance):
        return pltpu.roll(x, width * distance, 1)

    def from_above(x, distance):
        return pltpu.roll(x, LANES - width * distance, 1)

    rims = (
        from_below(items[22], 1),
        from_below(items[23], 1),
        from_above(items[20], 1),
        from_above(items[21], 1),
    )
    form = plain_form(items[:FORM], *rims)
    distance = 1
    while width * distance < LANES:
        form, unused = merge(form, [from_above(x, distance) for x in form])
        distance = 2 * distance
    unknown = [[None] * 5 for _ in range(4)]
    for x in range(4):
        k, a, b, c, d = form[5 * x : 5 * x + 5]
        unknown[x] = [c, d, a, b, k]
        unknown[x][x] = 1.0 + unknown[x][x]
    for pivot in range(4):
        inv = 1.0 / unknown[pivot][pivot]
        scaled = [unknown[pivot][c] * inv for c in range(pivot + 1, 5)]
        for x in range(4):
            if x == pivot:
                continue
            factor = unknown[x][pivot]
            for c in range(pivot + 1, 5):
                unknown[x][c] = unknown[x][c] - factor * scaled[c - pivot - 1]
        for c in range(pivot + 1, 5):
            unknown[pivot][c] = scaled[c - pivot - 1]
    p0, p1, l0, l1 = (unknown[x][4] for x in range(4))
    r0, r1 = from_above(p0, 1), from_above(p1, 1)
    terms = rim_terms([l0, l1, r0, r1], p0, from_above(l1, 1), *rims)
    square_ref[...] = jnp.zeros((LANES, LANES), jnp.float32)
    for x in range(4):
        square_ref[pl.ds(FIELDS * x, FIELDS), :] = terms[x]
    send_ref[...] = jnp.transpose(square_ref[...])


def xi_finish_kernel(
    got_ref, cols_ref, meet0_ref, meet1_ref, meet2_ref, right_ref,
    out_ref,
    square_ref, spread0_ref, spread1_ref, spread2_ref, solved_ref,
):
    square_ref[...] = jnp.transpose(got_ref[...])
    outside = [square_ref[pl.ds(FIELDS * x, FIELDS), :] for x in range(4)]
    spread_tree(
        outside, (meet0_ref, meet1_ref, meet2_ref), (spread0_ref, spread1_ref, spread2_ref)
    )
    for f in range(FIELDS):
        for j in range(STEPS):
            solved_ref[f, pl.ds(j, STEPS, stride=STEPS), :] = section_values(
                cols_ref, spread2_ref, f, j
            )
    apply_cells(right_ref, [solved_ref[g] for g in range(FIELDS)], out_ref)


def shape(*dims):
    return jax.ShapeDtypeStruct(dims, jnp.float32)


def vmem(*dims):
    return pltpu.VMEM(dims, jnp.float32)


KEPT = (
    shape(5, FIELDS, STEPS, STEPS, LANES),
    shape(FORM, 20, LANES),
    shape(FORM, 10, LANES),
    shape(FORM, 5, LANES),
)
FORMS = (vmem(FORM, 40, LANES), vmem(FORM, 20, LANES), vmem(FORM, 10, LANES))
SPREADS = (vmem(4, 10, LANES), vmem(4, 20, LANES), vmem(4, 40, LANES))


def call(kernel, outs, scratch, name, scalars=0):
    def run(*args):
        specs = [pl.BlockSpec(memory_space=pltpu.SMEM)] * scalars
        specs += [pl.BlockSpec(memory_space=pltpu.VMEM)] * (len(args) - scalars)
        out_specs = [pl.BlockSpec(memory_space=pltpu.VMEM)] * len(outs)
        return pl.pallas_call(
            kernel,
            out_shape=list(outs),
            in_specs=specs,
            out_specs=out_specs,
            scratch_shapes=list(scratch),
            compiler_params=pltpu.CompilerParams(vmem_limit_bytes=24 * 2**20),
            name=name,
        )(*args)

    return run


def per_device(residual, left_eta, middle, right_xi, speed_eta, speed_xi, damping_eta, damping_xi):
    fields, cells_xi, cells_local = residual.shape
    eta_send, *eta_kept = call(
        eta_reduce_kernel,
        (shape(SENT * FIELDS, LANES),) + KEPT,
        (vmem(FIELDS, cells_xi, LANES), vmem(2 * FIELDS + 1, LANES, LANES)) + FORMS,
        "eta_reduce",
    )(residual, left_eta, speed_eta, damping_eta)
    eta_got = lax.all_gather(eta_send, "eta", axis=0, tiled=True)
    place = lax.axis_index("eta").reshape(1).astype(jnp.int32)
    xi_send, *xi_kept = call(
        eta_finish_kernel,
        (shape(LANES, LANES),) + KEPT,
        FORMS
        + SPREADS
        + (
            vmem(4, 2, 40, LANES),
            vmem(4, FIELDS, LANES),
            vmem(FIELDS, LANES, LANES),
            vmem(FIELDS, cells_xi, LANES),
            vmem(LANES, LANES),
        ),
        "eta_finish",
        scalars=1,
    )(place, eta_got, *eta_kept, middle, speed_xi, damping_xi)
    loop = lax.axis_size("xi")
    xi_got = lax.all_to_all(
        xi_send.reshape(loop, LANES // loop, LANES), "xi", 0, 0, tiled=True
    ).reshape(LANES, LANES)
    (loop_send,) = call(xi_loop_kernel, (shape(LANES, LANES),), (vmem(LANES, LANES),), "xi_loop")(
        xi_got
    )
    loop_got = lax.all_to_all(
        loop_send.reshape(loop, LANES // loop, LANES), "xi", 0, 0, tiled=True
    ).reshape(LANES, LANES)
    (increment,) = call(
        xi_finish_kernel,
        (shape(fields, cells_xi, cells_local),),
        (vmem(LANES, LANES),) + SPREADS + (vmem(FIELDS, cells_xi, LANES),),
        "xi_finish",
    )(loop_got, *xi_kept, right_xi)
    return increment


def solution(mesh):
    in_specs = (
        P(None, "xi", "eta"),
        P(None, None, "xi", "eta"),
        P(None, None, "xi", "eta"),
        P(None, None, "xi", "eta"),
        P(None, "xi", "eta"),
        P(None, "xi", "eta"),
        P("xi", "eta"),
        P("xi", "eta"),
    )
    out_specs = P(None, "xi", "eta")
    return jax.shard_map(
        per_device, mesh=mesh, in_specs=in_specs, out_specs=out_specs, check_vma=False
    )
```

```python
import functools

import jax
import jax.numpy as jnp
from jax import lax
from jax.experimental import pallas as pl
from jax.experimental.pallas import tpu as pltpu
from jax.sharding import PartitionSpec as P

SPAN = 2
FIELDS = 5
STEPS = 8
LANES = 128
FORM = 20
SENT = 24


def merge(low, high):
    a_p0, a_p1, a_q0, a_q1 = (low[5 * x : 5 * x + 5] for x in range(4))
    b_p0, b_p1, b_q0, b_q1 = (high[5 * x : 5 * x + 5] for x in range(4))
    l00, l01, l10, l11 = b_p0[1], b_p0[2], b_p1[1], b_p1[2]
    u00, u01, u10, u11 = a_q0[3], a_q0[4], a_q1[3], a_q1[4]
    m00 = 1.0 - l00 * u00 - l01 * u10
    m01 = -(l00 * u01 + l01 * u11)
    m10 = -(l10 * u00 + l11 * u10)
    m11 = 1.0 - l10 * u01 - l11 * u11
    inv = 1.0 / (m00 * m11 - m01 * m10)
    m00, m01, m10, m11 = m00 * inv, m01 * inv, m10 * inv, m11 * inv
    r0 = [b_p0[0] - l00 * a_q0[0] - l01 * a_q1[0]]
    r1 = [b_p1[0] - l10 * a_q0[0] - l11 * a_q1[0]]
    for c in (1, 2):
        r0.append(-(l00 * a_q0[c] + l01 * a_q1[c]))
        r1.append(-(l10 * a_q0[c] + l11 * a_q1[c]))
    r0 += [b_p0[3], b_p0[4]]
    r1 += [b_p1[3], b_p1[4]]
    p0 = [m11 * s - m01 * t for s, t in zip(r0, r1)]
    p1 = [m00 * t - m10 * s for s, t in zip(r0, r1)]

    def through_p(row):
        out = [row[c] - row[3] * p0[c] - row[4] * p1[c] for c in (0, 1, 2)]
        return out + [-(row[3] * p0[c] + row[4] * p1[c]) for c in (3, 4)]

    q0, q1 = through_p(a_q0), through_p(a_q1)

    def through_q(row):
        out = [row[0] - row[1] * q0[0] - row[2] * q1[0]]
        out += [-(row[1] * q0[c] + row[2] * q1[c]) for c in (1, 2)]
        return out + [row[c] - row[1] * q0[c] - row[2] * q1[c] for c in (3, 4)]

    joined = through_p(a_p0) + through_p(a_p1) + through_q(b_q0) + through_q(b_q1)
    return joined, p0 + p1 + q0 + q1


def value_of(row, outside):
    return (row[0] - row[1] * outside[0] - row[2] * outside[1]) - (
        row[3] * outside[2] + row[4] * outside[3]
    )


def plain_form(form, damp_low, speed_low, damp_high, speed_high):
    turn_low = 2.0 * damp_low + 0.5 * speed_low
    turn_high = 0.5 * speed_high - 2.0 * damp_high
    rows = []
    for x in range(4):
        k, a, b, c, d = form[5 * x : 5 * x + 5]
        rows.append([k, a * damp_low, b - a * turn_low, c + d * turn_high, d * damp_high])
    first, last = rows[0], rows[3]
    e00, e01 = 1.0 + first[1], first[4]
    e10, e11 = last[1], 1.0 + last[4]
    inv = 1.0 / (e00 * e11 - e01 * e10)
    e00, e01, e10, e11 = e00 * inv, e01 * inv, e10 * inv, e11 * inv
    new_first = [e11 * s - e01 * t for s, t in zip(first, last)]
    new_last = [e00 * t - e10 * s for s, t in zip(first, last)]
    inner = [
        [row[c] - row[1] * new_first[c] - row[4] * new_last[c] for c in range(5)]
        for row in rows[1:3]
    ]
    return new_first + inner[0] + inner[1] + new_last


def rim_terms(outside, first, last, damp_low, speed_low, damp_high, speed_high):
    l0, l1, r0, r1 = outside
    low = damp_low * (l0 - 2.0 * l1 + first) - 0.5 * speed_low * l1
    high = damp_high * (last - 2.0 * r0 + r1) + 0.5 * speed_high * r0
    return [low, l1, r0, high]


def section_rows():
    return lax.broadcasted_iota(jnp.int32, (STEPS, LANES), 0)


def reduce_sections(values, speeds, damps, cols_ref, form_ref):
    row = section_rows()
    zero = jnp.zeros((STEPS, LANES), jnp.float32)

    def below(x):
        return jnp.where(row == 0, zero, pltpu.roll(x, 1, 0))

    def above(x):
        return jnp.where(row == STEPS - 1, zero, pltpu.roll(x, STEPS - 1, 0))

    damp = [damps(j) for j in range(STEPS)]
    damp = [below(damp[-1])] + damp + [above(damp[0])]
    edge = [2.0 * (damp[j] + damp[j + 1]) for j in range(STEPS + 1)]
    centre = [1.0 + damp[j] + 4.0 * damp[j + 1] + damp[j + 2] for j in range(STEPS)]
    far_first = jnp.where(row == 0, 1.0, damp[0])
    far_last = jnp.where(row == STEPS - 1, 1.0, damp[STEPS + 1])
    for f in range(FIELDS):
        half = [0.5 * speeds(f, j) for j in range(STEPS)]
        half = [below(half[-1])] + half + [above(half[0])]
        parts = []
        for j in range(STEPS):
            far_low = damp[j]
            near_low = -(half[j] + edge[j])
            near_up = half[j + 2] - edge[j + 1]
            far_up = far_last if j == STEPS - 1 else damp[j + 2]
            source = values(f, j)
            if j == 0:
                inv = 1.0 / centre[0]
                parts.append(
                    [source * inv, far_first * inv, near_low * inv, near_up * inv, far_up * inv]
                )
                continue
            k1, a1, b1, n1, m1 = parts[j - 1]
            if j == 1:
                inv = 1.0 / (centre[1] - near_low * n1)
                parts.append(
                    [
                        (source - near_low * k1) * inv,
                        -(near_low * a1) * inv,
                        (far_low - near_low * b1) * inv,
                        (near_up - near_low * m1) * inv,
                        far_up * inv,
                    ]
                )
                continue
            k2, a2, b2, n2, m2 = parts[j - 2]
            lead = near_low - far_low * n2
            inv = 1.0 / ((centre[j] - far_low * m2) - lead * n1)
            parts.append(
                [
                    ((source - far_low * k2) - lead * k1) * inv,
                    -(far_low * a2 + lead * a1) * inv,
                    -(far_low * b2 + lead * b1) * inv,
                    (near_up - lead * m1) * inv,
                    far_up * inv,
                ]
            )
        cols = [None] * STEPS
        cols[7] = parts[7]
        k, a, b, n, m = parts[6]
        nxt = cols[7]
        cols[6] = [
            k - n * nxt[0],
            a - n * nxt[1],
            b - n * nxt[2],
            m - n * nxt[3],
            -(n * nxt[4]),
        ]
        for j in range(STEPS - 3, -1, -1):
            k, a, b, n, m = parts[j]
            nxt, aft = cols[j + 1], cols[j + 2]
            cols[j] = [
                k - n * nxt[0] - m * aft[0],
                a - n * nxt[1] - m * aft[1],
                b - n * nxt[2] - m * aft[2],
                -(n * nxt[3] + m * aft[3]),
                -(n * nxt[4] + m * aft[4]),
            ]
        for j in range(STEPS):
            for c in range(5):
                cols_ref[c, f, j] = cols[j][c]
        for x, j in enumerate((0, 1, STEPS - 2, STEPS - 1)):
            for c in range(5):
                form_ref[5 * x + c, pl.ds(STEPS * f, STEPS), :] = cols[j][c]


def merge_rows(src_ref, count, meet_ref):
    low = [src_ref[v, pl.ds(0, count, stride=2), :] for v in range(FORM)]
    high = [src_ref[v, pl.ds(1, count, stride=2), :] for v in range(FORM)]
    joined, meet = merge(low, high)
    for v in range(FORM):
        meet_ref[v] = meet[v]
    return joined


def merge_tree(form_ref, mid_ref, small_ref, meets):
    for v, item in enumerate(merge_rows(form_ref, 20, meets[0])):
        mid_ref[v] = item
    for v, item in enumerate(merge_rows(mid_ref, 10, meets[1])):
        small_ref[v] = item
    return merge_rows(small_ref, 5, meets[2])


def spread_tree(outside, meets, spreads):
    for meet_ref, out_ref, count in zip(meets[::-1], spreads, (5, 10, 20)):
        p0, p1, q0, q1 = (
            value_of([meet_ref[5 * x + c] for c in range(5)], outside) for x in range(4)
        )
        even = (outside[0], outside[1], p0, p1)
        odd = (q0, q1, outside[2], outside[3])
        for x in range(4):
            out_ref[x, pl.ds(0, count, stride=2), :] = even[x]
            out_ref[x, pl.ds(1, count, stride=2), :] = odd[x]
        outside = [out_ref[x] for x in range(4)]


def section_values(cols_ref, spread_ref, f, j):
    outside = [spread_ref[x, pl.ds(STEPS * f, STEPS), :] for x in range(4)]
    return value_of([cols_ref[c, f, j] for c in range(5)], outside)


def mix(matrix_ref, f, values):
    total = matrix_ref[f, 0] * values[0]
    for g in range(1, FIELDS):
        total = total + matrix_ref[f, g] * values[g]
    return total


def to_eta_rows(block):
    beside = pltpu.roll(block, LANES - 1, 1)
    return jnp.transpose(jnp.concatenate([block, beside], axis=0))


def from_eta_rows(rows):
    both = jnp.transpose(rows)
    half = both.shape[0] // 2
    lane = lax.broadcasted_iota(jnp.int32, (half, LANES), 1)
    return jnp.where(lane % 2 == 0, both[:half], pltpu.roll(both[half:], 1, 1))


def eta_reduce_kernel(
    residual_hbm, left_hbm, speed_hbm, damp_hbm,
    send_ref, cols_ref, meet0_ref, meet1_ref, meet2_ref,
    residual_ref, left_ref, speed_ref, damp_ref, sems,
    turned_ref, form_ref, mid_ref, small_ref,
):
    copies = [
        pltpu.make_async_copy(damp_hbm, damp_ref, sems.at[0]),
        pltpu.make_async_copy(speed_hbm, speed_ref, sems.at[1]),
        pltpu.make_async_copy(residual_hbm, residual_ref, sems.at[2]),
        pltpu.make_async_copy(left_hbm, left_ref, sems.at[3]),
    ]
    for copy in copies:
        copy.start()
    copies[0].wait()
    turned_ref[2 * FIELDS] = to_eta_rows(damp_ref[...])
    copies[1].wait()
    for f in range(FIELDS):
        turned_ref[FIELDS + f] = to_eta_rows(speed_ref[f])
    copies[2].wait()
    copies[3].wait()
    for f in range(FIELDS):
        turned_ref[f] = to_eta_rows(mix(left_ref, f, [residual_ref[g] for g in range(FIELDS)]))

    def cell(index, j):
        return turned_ref[index, pl.ds(SPAN * j, STEPS, stride=SPAN * STEPS), :]

    reduce_sections(
        cell,
        lambda f, j: cell(FIELDS + f, j),
        lambda j: cell(2 * FIELDS, j),
        cols_ref,
        form_ref,
    )
    block = merge_tree(form_ref, mid_ref, small_ref, (meet0_ref, meet1_ref, meet2_ref))
    for v in range(FORM):
        send_ref[pl.ds(FIELDS * v, FIELDS), :] = block[v]
    final = SPAN * (STEPS * STEPS - 1)
    for f in range(FIELDS):
        rims = (
            turned_ref[2 * FIELDS, pl.ds(0, 1), :],
            turned_ref[FIELDS + f, pl.ds(0, 1), :],
            turned_ref[2 * FIELDS, pl.ds(final, 1), :],
            turned_ref[FIELDS + f, pl.ds(final, 1), :],
        )
        for r in range(4):
            send_ref[pl.ds(FIELDS * (FORM + r) + f, 1), :] = rims[r]


def eta_outside(place_ref, got_ref, form_ref, mid_ref, small_ref, meets, spreads, all_ref, own_ref):
    row = section_rows()
    zero = jnp.zeros((STEPS, LANES), jnp.float32)
    rows_each = SENT * FIELDS
    pair_forms, pair_meets, rims = [], [], []
    for f in range(FIELDS):
        halves = [
            [
                got_ref[pl.ds(rows_each * side + FIELDS * v + f, STEPS, stride=2 * rows_each), :]
                for v in range(SENT)
            ]
            for side in range(2)
        ]
        even, odd = halves
        rim_even = (
            jnp.where(row == 0, zero, pltpu.roll(odd[22], 1, 0)),
            jnp.where(row == 0, zero, pltpu.roll(odd[23], 1, 0)),
            odd[20],
            odd[21],
        )
        rim_odd = (
            even[22],
            even[23],
            jnp.where(row == STEPS - 1, zero, pltpu.roll(even[20], STEPS - 1, 0)),
            jnp.where(row == STEPS - 1, zero, pltpu.roll(even[21], STEPS - 1, 0)),
        )
        low = plain_form(even[:FORM], *rim_even)
        high = plain_form(odd[:FORM], *rim_odd)
        joined, meet = merge(low, high)
        for v in range(FORM):
            form_ref[v, pl.ds(STEPS * f, STEPS), :] = joined[v]
        pair_meets.append(meet)
        pair_forms.append((low[:5], low[15:], high[:5], high[15:]))
        rims.append((rim_even, rim_odd))
    merge_tree(form_ref, mid_ref, small_ref, meets)
    nothing = jnp.zeros((FIELDS, LANES), jnp.float32)
    spread_tree([nothing] * 4, meets, spreads)
    place = place_ref[0]
    for f in range(FIELDS):
        l0, l1, r0, r1 = (spreads[2][x, pl.ds(STEPS * f, STEPS), :] for x in range(4))
        p0, p1, q0, q1 = (
            value_of(pair_meets[f][5 * x : 5 * x + 5], (l0, l1, r0, r1)) for x in range(4)
        )
        for side, around in enumerate(((l0, l1, p0, p1), (q0, q1, r0, r1))):
            first = value_of(pair_forms[f][2 * side], around)
            last = value_of(pair_forms[f][2 * side + 1], around)
            for x, item in enumerate(rim_terms(around, first, last, *rims[f][side])):
                all_ref[x, side, pl.ds(STEPS * f, STEPS), :] = item
        side = lax.rem(place, 2)
        pair = lax.div(place, 2)
        for x in range(4):
            own_ref[x, pl.ds(f, 1), :] = all_ref[x, side, pl.ds(STEPS * f + pair, 1), :]


def eta_finish_kernel(
    place_ref, got_ref, eta_cols_ref, eta_meet0_ref, eta_meet1_ref, eta_meet2_ref,
    middle_ref, speed_ref, damp_ref,
    send_ref, cols_ref, meet0_ref, meet1_ref, meet2_ref,
    form_ref, mid_ref, small_ref, spread0_ref, spread1_ref, spread2_ref, all_ref, own_ref,
    turned_ref, mixed_ref, square_ref,
):
    spreads = (spread0_ref, spread1_ref, spread2_ref)
    meets = (meet0_ref, meet1_ref, meet2_ref)
    eta_outside(place_ref, got_ref, form_ref, mid_ref, small_ref, meets, spreads, all_ref, own_ref)
    spread_tree(
        [own_ref[x] for x in range(4)], (eta_meet0_ref, eta_meet1_ref, eta_meet2_ref), spreads
    )
    solved = []
    for f in range(FIELDS):
        for j in range(STEPS):
            turned_ref[f, pl.ds(SPAN * j, STEPS, stride=SPAN * STEPS), :] = section_values(
                eta_cols_ref, spread2_ref, f, j
            )
        solved.append(from_eta_rows(turned_ref[f]))
    for f in range(FIELDS):
        mixed_ref[f] = mix(middle_ref, f, solved)
    reduce_sections(
        lambda f, j: mixed_ref[f, pl.ds(j, STEPS, stride=STEPS), :],
        lambda f, j: speed_ref[f, pl.ds(j, STEPS, stride=STEPS), :],
        lambda j: damp_ref[pl.ds(j, STEPS, stride=STEPS), :],
        cols_ref,
        form_ref,
    )
    block = merge_tree(form_ref, mid_ref, small_ref, meets)
    for v in range(FORM):
        square_ref[pl.ds(FIELDS * v, FIELDS), :] = block[v]
    final = STEPS * STEPS - 1
    for f in range(FIELDS):
        rims = (
            damp_ref[pl.ds(0, 1), :],
            speed_ref[f, pl.ds(0, 1), :],
            damp_ref[pl.ds(final, 1), :],
            speed_ref[f, pl.ds(final, 1), :],
        )
        for r in range(4):
            square_ref[pl.ds(FIELDS * (FORM + r) + f, 1), :] = rims[r]
    square_ref[pl.ds(SENT * FIELDS, LANES - SENT * FIELDS), :] = jnp.zeros(
        (LANES - SENT * FIELDS, LANES), jnp.float32
    )
    send_ref[...] = jnp.transpose(square_ref[...])


def xi_loop_kernel(got_ref, send_ref, square_ref):
    square_ref[...] = jnp.transpose(got_ref[...])
    items = [square_ref[pl.ds(FIELDS * v, FIELDS), :] for v in range(SENT)]
    width = 4

    def from_below(x, distance):
        return pltpu.roll(x, width * distance, 1)

    def from_above(x, distance):
        return pltpu.roll(x, LANES - width * distance, 1)

    rims = (
        from_below(items[22], 1),
        from_below(items[23], 1),
        from_above(items[20], 1),
        from_above(items[21], 1),
    )
    form = plain_form(items[:FORM], *rims)
    distance = 1
    while width * distance < LANES:
        form, unused = merge(form, [from_above(x, distance) for x in form])
        distance = 2 * distance
    unknown = [[None] * 5 for _ in range(4)]
    for x in range(4):
        k, a, b, c, d = form[5 * x : 5 * x + 5]
        unknown[x] = [c, d, a, b, k]
        unknown[x][x] = 1.0 + unknown[x][x]
    for pivot in range(4):
        inv = 1.0 / unknown[pivot][pivot]
        scaled = [unknown[pivot][c] * inv for c in range(pivot + 1, 5)]
        for x in range(4):
            if x == pivot:
                continue
            factor = unknown[x][pivot]
            for c in range(pivot + 1, 5):
                unknown[x][c] = unknown[x][c] - factor * scaled[c - pivot - 1]
        for c in range(pivot + 1, 5):
            unknown[pivot][c] = scaled[c - pivot - 1]
    p0, p1, l0, l1 = (unknown[x][4] for x in range(4))
    r0, r1 = from_above(p0, 1), from_above(p1, 1)
    terms = rim_terms([l0, l1, r0, r1], p0, from_above(l1, 1), *rims)
    square_ref[...] = jnp.zeros((LANES, LANES), jnp.float32)
    for x in range(4):
        square_ref[pl.ds(FIELDS * x, FIELDS), :] = terms[x]
    square_ref[...] = jnp.transpose(square_ref[...])
    devices = LANES // width
    total = square_ref[pl.ds(0, devices, stride=width), :]
    for part in range(1, width):
        piece = square_ref[pl.ds(part, devices, stride=width), :]
        total = total + pltpu.roll(piece, part * devices, 1)
    send_ref[...] = total


def xi_finish_kernel(
    got_ref, cols_ref, meet0_ref, meet1_ref, meet2_ref, right_ref,
    out_hbm,
    square_ref, spread0_ref, spread1_ref, spread2_ref, solved_ref, out_ref, sems,
):
    devices = got_ref.shape[0]
    width = LANES // devices
    got = got_ref[...]
    square_ref[pl.ds(0, devices, stride=width), :] = got
    for part in range(1, width):
        square_ref[pl.ds(part, devices, stride=width), :] = pltpu.roll(
            got, LANES - part * devices, 1
        )
    square_ref[...] = jnp.transpose(square_ref[...])
    outside = [square_ref[pl.ds(FIELDS * x, FIELDS), :] for x in range(4)]
    spread_tree(
        outside, (meet0_ref, meet1_ref, meet2_ref), (spread0_ref, spread1_ref, spread2_ref)
    )
    for f in range(FIELDS):
        for j in range(STEPS):
            solved_ref[f, pl.ds(j, STEPS, stride=STEPS), :] = section_values(
                cols_ref, spread2_ref, f, j
            )
    copies = []
    for f in range(FIELDS):
        out_ref[f] = mix(right_ref, f, [solved_ref[g] for g in range(FIELDS)])
        copies.append(pltpu.make_async_copy(out_ref.at[f], out_hbm.at[f], sems.at[f]))
        copies[f].start()
    for copy in copies:
        copy.wait()


def shape(*dims):
    return jax.ShapeDtypeStruct(dims, jnp.float32)


def vmem(*dims):
    return pltpu.VMEM(dims, jnp.float32)


KEPT = (
    shape(5, FIELDS, STEPS, STEPS, LANES),
    shape(FORM, 20, LANES),
    shape(FORM, 10, LANES),
    shape(FORM, 5, LANES),
)
FORMS = (vmem(FORM, 40, LANES), vmem(FORM, 20, LANES), vmem(FORM, 10, LANES))
SPREADS = (vmem(4, 10, LANES), vmem(4, 20, LANES), vmem(4, 40, LANES))


ON_CHIP = pl.BlockSpec(memory_space=pltpu.VMEM)
IN_PLACE = pl.BlockSpec(memory_space=pltpu.HBM)


def call(kernel, in_specs, outs, out_specs, scratch, name):
    return pl.pallas_call(
        kernel,
        out_shape=list(outs),
        in_specs=in_specs,
        out_specs=out_specs,
        scratch_shapes=list(scratch),
        compiler_params=pltpu.CompilerParams(vmem_limit_bytes=24 * 2**20),
        name=name,
    )


def in_place(*arrays):
    return [pltpu.with_memory_space_constraint(x, pltpu.HBM) for x in arrays]


def eta_reduce(residual, left_eta, speed_eta, damping_eta):
    fields, cells_xi, _ = residual.shape
    return call(
        eta_reduce_kernel,
        [IN_PLACE] * 4,
        (shape(SENT * FIELDS, LANES),) + KEPT,
        [ON_CHIP] * 5,
        (
            vmem(fields, cells_xi, LANES),
            vmem(fields, fields, cells_xi, LANES),
            vmem(fields, cells_xi, LANES),
            vmem(cells_xi, LANES),
            pltpu.SemaphoreType.DMA((4,)),
            vmem(2 * FIELDS + 1, LANES, LANES),
        )
        + FORMS,
        "eta_reduce",
    )(*in_place(residual, left_eta, speed_eta, damping_eta))


def eta_finish(place, eta_got, eta_kept, middle, speed_xi, damping_xi):
    cells_xi = damping_xi.shape[0]
    return call(
        eta_finish_kernel,
        [pl.BlockSpec(memory_space=pltpu.SMEM)] + [ON_CHIP] * 8,
        (shape(LANES, LANES),) + KEPT,
        [ON_CHIP] * 5,
        FORMS
        + SPREADS
        + (
            vmem(4, 2, 40, LANES),
            vmem(4, FIELDS, LANES),
            vmem(FIELDS, LANES, LANES),
            vmem(FIELDS, cells_xi, LANES),
            vmem(LANES, LANES),
        ),
        "eta_finish",
    )(place, eta_got, *eta_kept, middle, speed_xi, damping_xi)


def xi_loop(xi_got, loop):
    return call(
        xi_loop_kernel,
        [ON_CHIP],
        (shape(loop, LANES),),
        [ON_CHIP],
        (vmem(LANES, LANES),),
        "xi_loop",
    )(xi_got)[0]


def xi_finish(loop_got, xi_kept, right_xi):
    fields, _, cells_xi, cells_local = right_xi.shape
    return call(
        xi_finish_kernel,
        [ON_CHIP] * 6,
        (shape(fields, cells_xi, cells_local),),
        [IN_PLACE],
        (vmem(LANES, LANES),)
        + SPREADS
        + (
            vmem(FIELDS, cells_xi, LANES),
            vmem(FIELDS, cells_xi, LANES),
            pltpu.SemaphoreType.DMA((FIELDS,)),
        ),
        "xi_finish",
    )(loop_got, *xi_kept, right_xi)[0]


def per_device(residual, left_eta, middle, right_xi, speed_eta, speed_xi, damping_eta, damping_xi):
    eta_send, *eta_kept = eta_reduce(residual, left_eta, speed_eta, damping_eta)
    eta_got = lax.all_gather(eta_send, "eta", axis=0, tiled=True)
    place = lax.axis_index("eta").reshape(1).astype(jnp.int32)
    xi_send, *xi_kept = eta_finish(place, eta_got, eta_kept, middle, speed_xi, damping_xi)
    loop = lax.axis_size("xi")
    xi_got = lax.all_to_all(
        xi_send.reshape(loop, LANES // loop, LANES), "xi", 0, 0, tiled=True
    ).reshape(LANES, LANES)
    loop_got = lax.all_to_all(
        xi_loop(xi_got, loop).reshape(loop, 1, LANES), "xi", 0, 0, tiled=True
    ).reshape(loop, LANES)
    return xi_finish(loop_got, xi_kept, right_xi)


def solution(mesh):
    in_specs = (
        P(None, "xi", "eta"),
        P(None, None, "xi", "eta"),
        P(None, None, "xi", "eta"),
        P(None, None, "xi", "eta"),
        P(None, "xi", "eta"),
        P(None, "xi", "eta"),
        P("xi", "eta"),
        P("xi", "eta"),
    )
    out_specs = P(None, "xi", "eta")
    return jax.shard_map(
        per_device, mesh=mesh, in_specs=in_specs, out_specs=out_specs, check_vma=False
    )
```

```python
import functools

import jax
import jax.numpy as jnp
from jax import lax
from jax.experimental import pallas as pl
from jax.experimental.pallas import tpu as pltpu
from jax.sharding import PartitionSpec as P

SPAN = 2
FIELDS = 5
STEPS = 8
LANES = 128
FORM = 20
SENT = 24


ROUNDING = 2.0**-24


def inverse_parts(m00, m01, m10, m11):
    both = m00 * m11
    determinant = both - m01 * m10
    inv = 1.0 / jnp.where(determinant == 0.0, both * ROUNDING, determinant)
    return m00 * inv, m01 * inv, m10 * inv, m11 * inv


def merge(low, high):
    a_p0, a_p1, a_q0, a_q1 = (low[5 * x : 5 * x + 5] for x in range(4))
    b_p0, b_p1, b_q0, b_q1 = (high[5 * x : 5 * x + 5] for x in range(4))
    l00, l01, l10, l11 = b_p0[1], b_p0[2], b_p1[1], b_p1[2]
    u00, u01, u10, u11 = a_q0[3], a_q0[4], a_q1[3], a_q1[4]
    m00 = 1.0 - l00 * u00 - l01 * u10
    m01 = -(l00 * u01 + l01 * u11)
    m10 = -(l10 * u00 + l11 * u10)
    m11 = 1.0 - l10 * u01 - l11 * u11
    m00, m01, m10, m11 = inverse_parts(m00, m01, m10, m11)
    r0 = [b_p0[0] - l00 * a_q0[0] - l01 * a_q1[0]]
    r1 = [b_p1[0] - l10 * a_q0[0] - l11 * a_q1[0]]
    for c in (1, 2):
        r0.append(-(l00 * a_q0[c] + l01 * a_q1[c]))
        r1.append(-(l10 * a_q0[c] + l11 * a_q1[c]))
    r0 += [b_p0[3], b_p0[4]]
    r1 += [b_p1[3], b_p1[4]]
    p0 = [m11 * s - m01 * t for s, t in zip(r0, r1)]
    p1 = [m00 * t - m10 * s for s, t in zip(r0, r1)]

    def through_p(row):
        out = [row[c] - row[3] * p0[c] - row[4] * p1[c] for c in (0, 1, 2)]
        return out + [-(row[3] * p0[c] + row[4] * p1[c]) for c in (3, 4)]

    q0, q1 = through_p(a_q0), through_p(a_q1)

    def through_q(row):
        out = [row[0] - row[1] * q0[0] - row[2] * q1[0]]
        out += [-(row[1] * q0[c] + row[2] * q1[c]) for c in (1, 2)]
        return out + [row[c] - row[1] * q0[c] - row[2] * q1[c] for c in (3, 4)]

    joined = through_p(a_p0) + through_p(a_p1) + through_q(b_q0) + through_q(b_q1)
    return joined, p0 + p1 + q0 + q1


def value_of(row, outside):
    return (row[0] - row[1] * outside[0] - row[2] * outside[1]) - (
        row[3] * outside[2] + row[4] * outside[3]
    )


def plain_form(form, damp_low, speed_low, damp_high, speed_high):
    turn_low = 2.0 * damp_low + 0.5 * speed_low
    turn_high = 0.5 * speed_high - 2.0 * damp_high
    rows = []
    for x in range(4):
        k, a, b, c, d = form[5 * x : 5 * x + 5]
        rows.append([k, a * damp_low, b - a * turn_low, c + d * turn_high, d * damp_high])
    first, last = rows[0], rows[3]
    e00, e01 = 1.0 + first[1], first[4]
    e10, e11 = last[1], 1.0 + last[4]
    e00, e01, e10, e11 = inverse_parts(e00, e01, e10, e11)
    new_first = [e11 * s - e01 * t for s, t in zip(first, last)]
    new_last = [e00 * t - e10 * s for s, t in zip(first, last)]
    inner = [
        [row[c] - row[1] * new_first[c] - row[4] * new_last[c] for c in range(5)]
        for row in rows[1:3]
    ]
    return new_first + inner[0] + inner[1] + new_last


def rim_terms(outside, first, last, damp_low, speed_low, damp_high, speed_high):
    l0, l1, r0, r1 = outside
    low = damp_low * (l0 - 2.0 * l1 + first) - 0.5 * speed_low * l1
    high = damp_high * (last - 2.0 * r0 + r1) + 0.5 * speed_high * r0
    return [low, l1, r0, high]


def section_rows():
    return lax.broadcasted_iota(jnp.int32, (STEPS, LANES), 0)


def reduce_sections(values, speeds, damps, cols_ref, form_ref):
    row = section_rows()
    zero = jnp.zeros((STEPS, LANES), jnp.float32)

    def below(x):
        return jnp.where(row == 0, zero, pltpu.roll(x, 1, 0))

    def above(x):
        return jnp.where(row == STEPS - 1, zero, pltpu.roll(x, STEPS - 1, 0))

    damp = [damps(j) for j in range(STEPS)]
    damp = [below(damp[-1])] + damp + [above(damp[0])]
    edge = [2.0 * (damp[j] + damp[j + 1]) for j in range(STEPS + 1)]
    centre = [1.0 + damp[j] + 4.0 * damp[j + 1] + damp[j + 2] for j in range(STEPS)]
    far_first = jnp.where(row == 0, 1.0, damp[0])
    far_last = jnp.where(row == STEPS - 1, 1.0, damp[STEPS + 1])
    for f in range(FIELDS):
        half = [0.5 * speeds(f, j) for j in range(STEPS)]
        half = [below(half[-1])] + half + [above(half[0])]
        parts = []
        for j in range(STEPS):
            far_low = damp[j]
            near_low = -(half[j] + edge[j])
            near_up = half[j + 2] - edge[j + 1]
            far_up = far_last if j == STEPS - 1 else damp[j + 2]
            source = values(f, j)
            if j == 0:
                inv = 1.0 / centre[0]
                parts.append(
                    [source * inv, far_first * inv, near_low * inv, near_up * inv, far_up * inv]
                )
                continue
            k1, a1, b1, n1, m1 = parts[j - 1]
            if j == 1:
                inv = 1.0 / (centre[1] - near_low * n1)
                parts.append(
                    [
                        (source - near_low * k1) * inv,
                        -(near_low * a1) * inv,
                        (far_low - near_low * b1) * inv,
                        (near_up - near_low * m1) * inv,
                        far_up * inv,
                    ]
                )
                continue
            k2, a2, b2, n2, m2 = parts[j - 2]
            lead = near_low - far_low * n2
            inv = 1.0 / ((centre[j] - far_low * m2) - lead * n1)
            parts.append(
                [
                    ((source - far_low * k2) - lead * k1) * inv,
                    -(far_low * a2 + lead * a1) * inv,
                    -(far_low * b2 + lead * b1) * inv,
                    (near_up - lead * m1) * inv,
                    far_up * inv,
                ]
            )
        cols = [None] * STEPS
        cols[7] = parts[7]
        k, a, b, n, m = parts[6]
        nxt = cols[7]
        cols[6] = [
            k - n * nxt[0],
            a - n * nxt[1],
            b - n * nxt[2],
            m - n * nxt[3],
            -(n * nxt[4]),
        ]
        for j in range(STEPS - 3, -1, -1):
            k, a, b, n, m = parts[j]
            nxt, aft = cols[j + 1], cols[j + 2]
            cols[j] = [
                k - n * nxt[0] - m * aft[0],
                a - n * nxt[1] - m * aft[1],
                b - n * nxt[2] - m * aft[2],
                -(n * nxt[3] + m * aft[3]),
                -(n * nxt[4] + m * aft[4]),
            ]
        for j in range(STEPS):
            for c in range(5):
                cols_ref[c, f, j] = cols[j][c]
        for x, j in enumerate((0, 1, STEPS - 2, STEPS - 1)):
            for c in range(5):
                form_ref[5 * x + c, pl.ds(STEPS * f, STEPS), :] = cols[j][c]


def merge_rows(src_ref, count, meet_ref):
    low = [src_ref[v, pl.ds(0, count, stride=2), :] for v in range(FORM)]
    high = [src_ref[v, pl.ds(1, count, stride=2), :] for v in range(FORM)]
    joined, meet = merge(low, high)
    for v in range(FORM):
        meet_ref[v] = meet[v]
    return joined


def merge_tree(form_ref, mid_ref, small_ref, meets):
    for v, item in enumerate(merge_rows(form_ref, 20, meets[0])):
        mid_ref[v] = item
    for v, item in enumerate(merge_rows(mid_ref, 10, meets[1])):
        small_ref[v] = item
    return merge_rows(small_ref, 5, meets[2])


def spread_tree(outside, meets, spreads):
    for meet_ref, out_ref, count in zip(meets[::-1], spreads, (5, 10, 20)):
        p0, p1, q0, q1 = (
            value_of([meet_ref[5 * x + c] for c in range(5)], outside) for x in range(4)
        )
        even = (outside[0], outside[1], p0, p1)
        odd = (q0, q1, outside[2], outside[3])
        for x in range(4):
            out_ref[x, pl.ds(0, count, stride=2), :] = even[x]
            out_ref[x, pl.ds(1, count, stride=2), :] = odd[x]
        outside = [out_ref[x] for x in range(4)]


def section_values(cols_ref, spread_ref, f, j):
    outside = [spread_ref[x, pl.ds(STEPS * f, STEPS), :] for x in range(4)]
    return value_of([cols_ref[c, f, j] for c in range(5)], outside)


def mix(matrix_ref, f, values):
    total = matrix_ref[f, 0] * values[0]
    for g in range(1, FIELDS):
        total = total + matrix_ref[f, g] * values[g]
    return total


def to_eta_rows(block):
    beside = pltpu.roll(block, LANES - 1, 1)
    return jnp.transpose(jnp.concatenate([block, beside], axis=0))


def from_eta_rows(rows):
    both = jnp.transpose(rows)
    half = both.shape[0] // 2
    lane = lax.broadcasted_iota(jnp.int32, (half, LANES), 1)
    return jnp.where(lane % 2 == 0, both[:half], pltpu.roll(both[half:], 1, 1))


def eta_reduce_kernel(
    residual_hbm, left_hbm, speed_hbm, damp_hbm,
    send_ref, cols_ref, meet0_ref, meet1_ref, meet2_ref,
    residual_ref, left_ref, speed_ref, damp_ref, sems,
    turned_ref, form_ref, mid_ref, small_ref,
):
    copies = [
        pltpu.make_async_copy(damp_hbm, damp_ref, sems.at[0]),
        pltpu.make_async_copy(speed_hbm, speed_ref, sems.at[1]),
        pltpu.make_async_copy(residual_hbm, residual_ref, sems.at[2]),
        pltpu.make_async_copy(left_hbm, left_ref, sems.at[3]),
    ]
    for copy in copies:
        copy.start()
    copies[0].wait()
    turned_ref[2 * FIELDS] = to_eta_rows(damp_ref[...])
    copies[1].wait()
    for f in range(FIELDS):
        turned_ref[FIELDS + f] = to_eta_rows(speed_ref[f])
    copies[2].wait()
    copies[3].wait()
    for f in range(FIELDS):
        turned_ref[f] = to_eta_rows(mix(left_ref, f, [residual_ref[g] for g in range(FIELDS)]))

    def cell(index, j):
        return turned_ref[index, pl.ds(SPAN * j, STEPS, stride=SPAN * STEPS), :]

    reduce_sections(
        cell,
        lambda f, j: cell(FIELDS + f, j),
        lambda j: cell(2 * FIELDS, j),
        cols_ref,
        form_ref,
    )
    block = merge_tree(form_ref, mid_ref, small_ref, (meet0_ref, meet1_ref, meet2_ref))
    for v in range(FORM):
        send_ref[pl.ds(FIELDS * v, FIELDS), :] = block[v]
    final = SPAN * (STEPS * STEPS - 1)
    for f in range(FIELDS):
        rims = (
            turned_ref[2 * FIELDS, pl.ds(0, 1), :],
            turned_ref[FIELDS + f, pl.ds(0, 1), :],
            turned_ref[2 * FIELDS, pl.ds(final, 1), :],
            turned_ref[FIELDS + f, pl.ds(final, 1), :],
        )
        for r in range(4):
            send_ref[pl.ds(FIELDS * (FORM + r) + f, 1), :] = rims[r]


def eta_outside(place_ref, got_ref, form_ref, mid_ref, small_ref, meets, spreads, all_ref, own_ref):
    row = section_rows()
    zero = jnp.zeros((STEPS, LANES), jnp.float32)
    rows_each = SENT * FIELDS
    pair_forms, pair_meets, rims = [], [], []
    for f in range(FIELDS):
        halves = [
            [
                got_ref[pl.ds(rows_each * side + FIELDS * v + f, STEPS, stride=2 * rows_each), :]
                for v in range(SENT)
            ]
            for side in range(2)
        ]
        even, odd = halves
        rim_even = (
            jnp.where(row == 0, zero, pltpu.roll(odd[22], 1, 0)),
            jnp.where(row == 0, zero, pltpu.roll(odd[23], 1, 0)),
            odd[20],
            odd[21],
        )
        rim_odd = (
            even[22],
            even[23],
            jnp.where(row == STEPS - 1, zero, pltpu.roll(even[20], STEPS - 1, 0)),
            jnp.where(row == STEPS - 1, zero, pltpu.roll(even[21], STEPS - 1, 0)),
        )
        low = plain_form(even[:FORM], *rim_even)
        high = plain_form(odd[:FORM], *rim_odd)
        joined, meet = merge(low, high)
        for v in range(FORM):
            form_ref[v, pl.ds(STEPS * f, STEPS), :] = joined[v]
        pair_meets.append(meet)
        pair_forms.append((low[:5], low[15:], high[:5], high[15:]))
        rims.append((rim_even, rim_odd))
    merge_tree(form_ref, mid_ref, small_ref, meets)
    nothing = jnp.zeros((FIELDS, LANES), jnp.float32)
    spread_tree([nothing] * 4, meets, spreads)
    place = place_ref[0]
    for f in range(FIELDS):
        l0, l1, r0, r1 = (spreads[2][x, pl.ds(STEPS * f, STEPS), :] for x in range(4))
        p0, p1, q0, q1 = (
            value_of(pair_meets[f][5 * x : 5 * x + 5], (l0, l1, r0, r1)) for x in range(4)
        )
        for side, around in enumerate(((l0, l1, p0, p1), (q0, q1, r0, r1))):
            first = value_of(pair_forms[f][2 * side], around)
            last = value_of(pair_forms[f][2 * side + 1], around)
            for x, item in enumerate(rim_terms(around, first, last, *rims[f][side])):
                all_ref[x, side, pl.ds(STEPS * f, STEPS), :] = item
        side = lax.rem(place, 2)
        pair = lax.div(place, 2)
        for x in range(4):
            own_ref[x, pl.ds(f, 1), :] = all_ref[x, side, pl.ds(STEPS * f + pair, 1), :]


def eta_finish_kernel(
    place_ref, got_ref, eta_cols_ref, eta_meet0_ref, eta_meet1_ref, eta_meet2_ref,
    middle_ref, speed_ref, damp_ref,
    send_ref, cols_ref, meet0_ref, meet1_ref, meet2_ref,
    form_ref, mid_ref, small_ref, spread0_ref, spread1_ref, spread2_ref, all_ref, own_ref,
    turned_ref, mixed_ref, square_ref,
):
    spreads = (spread0_ref, spread1_ref, spread2_ref)
    meets = (meet0_ref, meet1_ref, meet2_ref)
    eta_outside(place_ref, got_ref, form_ref, mid_ref, small_ref, meets, spreads, all_ref, own_ref)
    spread_tree(
        [own_ref[x] for x in range(4)], (eta_meet0_ref, eta_meet1_ref, eta_meet2_ref), spreads
    )
    solved = []
    for f in range(FIELDS):
        for j in range(STEPS):
            turned_ref[f, pl.ds(SPAN * j, STEPS, stride=SPAN * STEPS), :] = section_values(
                eta_cols_ref, spread2_ref, f, j
            )
        solved.append(from_eta_rows(turned_ref[f]))
    for f in range(FIELDS):
        mixed_ref[f] = mix(middle_ref, f, solved)
    reduce_sections(
        lambda f, j: mixed_ref[f, pl.ds(j, STEPS, stride=STEPS), :],
        lambda f, j: speed_ref[f, pl.ds(j, STEPS, stride=STEPS), :],
        lambda j: damp_ref[pl.ds(j, STEPS, stride=STEPS), :],
        cols_ref,
        form_ref,
    )
    block = merge_tree(form_ref, mid_ref, small_ref, meets)
    for v in range(FORM):
        square_ref[pl.ds(FIELDS * v, FIELDS), :] = block[v]
    final = STEPS * STEPS - 1
    for f in range(FIELDS):
        rims = (
            damp_ref[pl.ds(0, 1), :],
            speed_ref[f, pl.ds(0, 1), :],
            damp_ref[pl.ds(final, 1), :],
            speed_ref[f, pl.ds(final, 1), :],
        )
        for r in range(4):
            square_ref[pl.ds(FIELDS * (FORM + r) + f, 1), :] = rims[r]
    square_ref[pl.ds(SENT * FIELDS, LANES - SENT * FIELDS), :] = jnp.zeros(
        (LANES - SENT * FIELDS, LANES), jnp.float32
    )
    send_ref[...] = jnp.transpose(square_ref[...])


def xi_loop_kernel(got_ref, send_ref, square_ref):
    square_ref[...] = jnp.transpose(got_ref[...])
    items = [square_ref[pl.ds(FIELDS * v, FIELDS), :] for v in range(SENT)]
    width = 4

    def from_below(x, distance):
        return pltpu.roll(x, width * distance, 1)

    def from_above(x, distance):
        return pltpu.roll(x, LANES - width * distance, 1)

    rims = (
        from_below(items[22], 1),
        from_below(items[23], 1),
        from_above(items[20], 1),
        from_above(items[21], 1),
    )
    form = plain_form(items[:FORM], *rims)
    distance = 1
    while width * distance < LANES:
        form, unused = merge(form, [from_above(x, distance) for x in form])
        distance = 2 * distance
    rows = [form[5 * x : 5 * x + 5] for x in range(4)]
    e00, e01, e10, e11 = inverse_parts(
        1.0 + rows[0][3], rows[0][4], rows[1][3], 1.0 + rows[1][4]
    )
    first = [e11 * rows[0][c] - e01 * rows[1][c] for c in range(3)]
    second = [e00 * rows[1][c] - e10 * rows[0][c] for c in range(3)]
    left = [
        [row[c] - row[3] * first[c] - row[4] * second[c] for c in range(3)] for row in rows[2:]
    ]
    e00, e01, e10, e11 = inverse_parts(
        1.0 + left[0][1], left[0][2], left[1][1], 1.0 + left[1][2]
    )
    l0 = e11 * left[0][0] - e01 * left[1][0]
    l1 = e00 * left[1][0] - e10 * left[0][0]
    p0 = first[0] - first[1] * l0 - first[2] * l1
    p1 = second[0] - second[1] * l0 - second[2] * l1
    r0, r1 = from_above(p0, 1), from_above(p1, 1)
    terms = rim_terms([l0, l1, r0, r1], p0, from_above(l1, 1), *rims)
    square_ref[...] = jnp.zeros((LANES, LANES), jnp.float32)
    for x in range(4):
        square_ref[pl.ds(FIELDS * x, FIELDS), :] = terms[x]
    square_ref[...] = jnp.transpose(square_ref[...])
    devices = LANES // width
    total = square_ref[pl.ds(0, devices, stride=width), :]
    for part in range(1, width):
        piece = square_ref[pl.ds(part, devices, stride=width), :]
        total = total + pltpu.roll(piece, part * devices, 1)
    send_ref[...] = total


def xi_finish_kernel(
    got_ref, cols_ref, meet0_ref, meet1_ref, meet2_ref, right_ref,
    out_hbm,
    square_ref, spread0_ref, spread1_ref, spread2_ref, solved_ref, out_ref, sems,
):
    devices = got_ref.shape[0]
    width = LANES // devices
    got = got_ref[...]
    square_ref[pl.ds(0, devices, stride=width), :] = got
    for part in range(1, width):
        square_ref[pl.ds(part, devices, stride=width), :] = pltpu.roll(
            got, LANES - part * devices, 1
        )
    square_ref[...] = jnp.transpose(square_ref[...])
    outside = [square_ref[pl.ds(FIELDS * x, FIELDS), :] for x in range(4)]
    spread_tree(
        outside, (meet0_ref, meet1_ref, meet2_ref), (spread0_ref, spread1_ref, spread2_ref)
    )
    for f in range(FIELDS):
        for j in range(STEPS):
            solved_ref[f, pl.ds(j, STEPS, stride=STEPS), :] = section_values(
                cols_ref, spread2_ref, f, j
            )
    copies = []
    for f in range(FIELDS):
        out_ref[f] = mix(right_ref, f, [solved_ref[g] for g in range(FIELDS)])
        copies.append(pltpu.make_async_copy(out_ref.at[f], out_hbm.at[f], sems.at[f]))
        copies[f].start()
    for copy in copies:
        copy.wait()


def shape(*dims):
    return jax.ShapeDtypeStruct(dims, jnp.float32)


def vmem(*dims):
    return pltpu.VMEM(dims, jnp.float32)


KEPT = (
    shape(5, FIELDS, STEPS, STEPS, LANES),
    shape(FORM, 20, LANES),
    shape(FORM, 10, LANES),
    shape(FORM, 5, LANES),
)
FORMS = (vmem(FORM, 40, LANES), vmem(FORM, 20, LANES), vmem(FORM, 10, LANES))
SPREADS = (vmem(4, 10, LANES), vmem(4, 20, LANES), vmem(4, 40, LANES))


ON_CHIP = pl.BlockSpec(memory_space=pltpu.VMEM)
IN_PLACE = pl.BlockSpec(memory_space=pltpu.HBM)


def call(kernel, in_specs, outs, out_specs, scratch, name):
    return pl.pallas_call(
        kernel,
        out_shape=list(outs),
        in_specs=in_specs,
        out_specs=out_specs,
        scratch_shapes=list(scratch),
        compiler_params=pltpu.CompilerParams(vmem_limit_bytes=24 * 2**20),
        name=name,
    )


def in_place(*arrays):
    return [pltpu.with_memory_space_constraint(x, pltpu.HBM) for x in arrays]


def eta_reduce(residual, left_eta, speed_eta, damping_eta):
    fields, cells_xi, _ = residual.shape
    return call(
        eta_reduce_kernel,
        [IN_PLACE] * 4,
        (shape(SENT * FIELDS, LANES),) + KEPT,
        [ON_CHIP] * 5,
        (
            vmem(fields, cells_xi, LANES),
            vmem(fields, fields, cells_xi, LANES),
            vmem(fields, cells_xi, LANES),
            vmem(cells_xi, LANES),
            pltpu.SemaphoreType.DMA((4,)),
            vmem(2 * FIELDS + 1, LANES, LANES),
        )
        + FORMS,
        "eta_reduce",
    )(*in_place(residual, left_eta, speed_eta, damping_eta))


def eta_finish(place, eta_got, eta_kept, middle, speed_xi, damping_xi):
    cells_xi = damping_xi.shape[0]
    return call(
        eta_finish_kernel,
        [pl.BlockSpec(memory_space=pltpu.SMEM)] + [ON_CHIP] * 8,
        (shape(LANES, LANES),) + KEPT,
        [ON_CHIP] * 5,
        FORMS
        + SPREADS
        + (
            vmem(4, 2, 40, LANES),
            vmem(4, FIELDS, LANES),
            vmem(FIELDS, LANES, LANES),
            vmem(FIELDS, cells_xi, LANES),
            vmem(LANES, LANES),
        ),
        "eta_finish",
    )(place, eta_got, *eta_kept, middle, speed_xi, damping_xi)


def xi_loop(xi_got, loop):
    return call(
        xi_loop_kernel,
        [ON_CHIP],
        (shape(loop, LANES),),
        [ON_CHIP],
        (vmem(LANES, LANES),),
        "xi_loop",
    )(xi_got)[0]


def xi_finish(loop_got, xi_kept, right_xi):
    fields, _, cells_xi, cells_local = right_xi.shape
    return call(
        xi_finish_kernel,
        [ON_CHIP] * 6,
        (shape(fields, cells_xi, cells_local),),
        [IN_PLACE],
        (vmem(LANES, LANES),)
        + SPREADS
        + (
            vmem(FIELDS, cells_xi, LANES),
            vmem(FIELDS, cells_xi, LANES),
            pltpu.SemaphoreType.DMA((FIELDS,)),
        ),
        "xi_finish",
    )(loop_got, *xi_kept, right_xi)[0]


def per_device(residual, left_eta, middle, right_xi, speed_eta, speed_xi, damping_eta, damping_xi):
    eta_send, *eta_kept = eta_reduce(residual, left_eta, speed_eta, damping_eta)
    eta_got = lax.all_gather(eta_send, "eta", axis=0, tiled=True)
    place = lax.axis_index("eta").reshape(1).astype(jnp.int32)
    xi_send, *xi_kept = eta_finish(place, eta_got, eta_kept, middle, speed_xi, damping_xi)
    loop = lax.axis_size("xi")
    xi_got = lax.all_to_all(
        xi_send.reshape(loop, LANES // loop, LANES), "xi", 0, 0, tiled=True
    ).reshape(LANES, LANES)
    loop_got = lax.all_to_all(
        xi_loop(xi_got, loop).reshape(loop, 1, LANES), "xi", 0, 0, tiled=True
    ).reshape(loop, LANES)
    return xi_finish(loop_got, xi_kept, right_xi)


def solution(mesh):
    in_specs = (
        P(None, "xi", "eta"),
        P(None, None, "xi", "eta"),
        P(None, None, "xi", "eta"),
        P(None, None, "xi", "eta"),
        P(None, "xi", "eta"),
        P(None, "xi", "eta"),
        P("xi", "eta"),
        P("xi", "eta"),
    )
    out_specs = P(None, "xi", "eta")
    return jax.shard_map(
        per_device, mesh=mesh, in_specs=in_specs, out_specs=out_specs, check_vma=False
    )
```

```python
import functools

import jax
import jax.numpy as jnp
from jax import lax
from jax.experimental import pallas as pl
from jax.experimental.pallas import tpu as pltpu
from jax.sharding import PartitionSpec as P

SPAN = 2
FIELDS = 5
STEPS = 8
LANES = 128
FORM = 20
SENT = 24


ROUNDING = 2.0**-24


def inverse_parts(m00, m01, m10, m11):
    both = m00 * m11
    determinant = both - m01 * m10
    inv = 1.0 / jnp.where(determinant == 0.0, both * ROUNDING, determinant)
    return m00 * inv, m01 * inv, m10 * inv, m11 * inv


def merge(low, high):
    a_p0, a_p1, a_q0, a_q1 = (low[5 * x : 5 * x + 5] for x in range(4))
    b_p0, b_p1, b_q0, b_q1 = (high[5 * x : 5 * x + 5] for x in range(4))
    l00, l01, l10, l11 = b_p0[1], b_p0[2], b_p1[1], b_p1[2]
    u00, u01, u10, u11 = a_q0[3], a_q0[4], a_q1[3], a_q1[4]
    m00 = 1.0 - l00 * u00 - l01 * u10
    m01 = -(l00 * u01 + l01 * u11)
    m10 = -(l10 * u00 + l11 * u10)
    m11 = 1.0 - l10 * u01 - l11 * u11
    m00, m01, m10, m11 = inverse_parts(m00, m01, m10, m11)
    r0 = [b_p0[0] - l00 * a_q0[0] - l01 * a_q1[0]]
    r1 = [b_p1[0] - l10 * a_q0[0] - l11 * a_q1[0]]
    for c in (1, 2):
        r0.append(-(l00 * a_q0[c] + l01 * a_q1[c]))
        r1.append(-(l10 * a_q0[c] + l11 * a_q1[c]))
    r0 += [b_p0[3], b_p0[4]]
    r1 += [b_p1[3], b_p1[4]]
    p0 = [m11 * s - m01 * t for s, t in zip(r0, r1)]
    p1 = [m00 * t - m10 * s for s, t in zip(r0, r1)]

    def through_p(row):
        out = [row[c] - row[3] * p0[c] - row[4] * p1[c] for c in (0, 1, 2)]
        return out + [-(row[3] * p0[c] + row[4] * p1[c]) for c in (3, 4)]

    q0, q1 = through_p(a_q0), through_p(a_q1)

    def through_q(row):
        out = [row[0] - row[1] * q0[0] - row[2] * q1[0]]
        out += [-(row[1] * q0[c] + row[2] * q1[c]) for c in (1, 2)]
        return out + [row[c] - row[1] * q0[c] - row[2] * q1[c] for c in (3, 4)]

    joined = through_p(a_p0) + through_p(a_p1) + through_q(b_q0) + through_q(b_q1)
    return joined, p0 + p1 + q0 + q1


def value_of(row, outside):
    return (row[0] - row[1] * outside[0] - row[2] * outside[1]) - (
        row[3] * outside[2] + row[4] * outside[3]
    )


def plain_form(form, damp_low, speed_low, damp_high, speed_high):
    turn_low = 2.0 * damp_low + 0.5 * speed_low
    turn_high = 0.5 * speed_high - 2.0 * damp_high
    rows = []
    for x in range(4):
        k, a, b, c, d = form[5 * x : 5 * x + 5]
        rows.append([k, a * damp_low, b - a * turn_low, c + d * turn_high, d * damp_high])
    first, last = rows[0], rows[3]
    e00, e01 = 1.0 + first[1], first[4]
    e10, e11 = last[1], 1.0 + last[4]
    e00, e01, e10, e11 = inverse_parts(e00, e01, e10, e11)
    new_first = [e11 * s - e01 * t for s, t in zip(first, last)]
    new_last = [e00 * t - e10 * s for s, t in zip(first, last)]
    inner = [
        [row[c] - row[1] * new_first[c] - row[4] * new_last[c] for c in range(5)]
        for row in rows[1:3]
    ]
    return new_first + inner[0] + inner[1] + new_last


def rim_terms(outside, first, last, damp_low, speed_low, damp_high, speed_high):
    l0, l1, r0, r1 = outside
    low = damp_low * (l0 - 2.0 * l1 + first) - 0.5 * speed_low * l1
    high = damp_high * (last - 2.0 * r0 + r1) + 0.5 * speed_high * r0
    return [low, l1, r0, high]


def section_rows():
    return lax.broadcasted_iota(jnp.int32, (STEPS, LANES), 0)


def reduce_sections(values, speeds, damps, cols_ref, form_ref):
    row = section_rows()
    zero = jnp.zeros((STEPS, LANES), jnp.float32)

    def below(x):
        return jnp.where(row == 0, zero, pltpu.roll(x, 1, 0))

    def above(x):
        return jnp.where(row == STEPS - 1, zero, pltpu.roll(x, STEPS - 1, 0))

    damp = [damps(j) for j in range(STEPS)]
    damp = [below(damp[-1])] + damp + [above(damp[0])]
    edge = [2.0 * (damp[j] + damp[j + 1]) for j in range(STEPS + 1)]
    centre = [1.0 + damp[j] + 4.0 * damp[j + 1] + damp[j + 2] for j in range(STEPS)]
    far_first = jnp.where(row == 0, 1.0, damp[0])
    far_last = jnp.where(row == STEPS - 1, 1.0, damp[STEPS + 1])
    for f in range(FIELDS):
        half = [0.5 * speeds(f, j) for j in range(STEPS)]
        half = [below(half[-1])] + half + [above(half[0])]
        parts = []
        for j in range(STEPS):
            far_low = damp[j]
            near_low = -(half[j] + edge[j])
            near_up = half[j + 2] - edge[j + 1]
            far_up = far_last if j == STEPS - 1 else damp[j + 2]
            source = values(f, j)
            if j == 0:
                inv = 1.0 / centre[0]
                parts.append(
                    [source * inv, far_first * inv, near_low * inv, near_up * inv, far_up * inv]
                )
                continue
            k1, a1, b1, n1, m1 = parts[j - 1]
            if j == 1:
                inv = 1.0 / (centre[1] - near_low * n1)
                parts.append(
                    [
                        (source - near_low * k1) * inv,
                        -(near_low * a1) * inv,
                        (far_low - near_low * b1) * inv,
                        (near_up - near_low * m1) * inv,
                        far_up * inv,
                    ]
                )
                continue
            k2, a2, b2, n2, m2 = parts[j - 2]
            lead = near_low - far_low * n2
            inv = 1.0 / ((centre[j] - far_low * m2) - lead * n1)
            parts.append(
                [
                    ((source - far_low * k2) - lead * k1) * inv,
                    -(far_low * a2 + lead * a1) * inv,
                    -(far_low * b2 + lead * b1) * inv,
                    (near_up - lead * m1) * inv,
                    far_up * inv,
                ]
            )
        cols = [None] * STEPS
        cols[7] = parts[7]
        k, a, b, n, m = parts[6]
        nxt = cols[7]
        cols[6] = [
            k - n * nxt[0],
            a - n * nxt[1],
            b - n * nxt[2],
            m - n * nxt[3],
            -(n * nxt[4]),
        ]
        for j in range(STEPS - 3, -1, -1):
            k, a, b, n, m = parts[j]
            nxt, aft = cols[j + 1], cols[j + 2]
            cols[j] = [
                k - n * nxt[0] - m * aft[0],
                a - n * nxt[1] - m * aft[1],
                b - n * nxt[2] - m * aft[2],
                -(n * nxt[3] + m * aft[3]),
                -(n * nxt[4] + m * aft[4]),
            ]
        for j in range(STEPS):
            for c in range(5):
                cols_ref[c, f, j] = cols[j][c]
        for x, j in enumerate((0, 1, STEPS - 2, STEPS - 1)):
            for c in range(5):
                form_ref[5 * x + c, pl.ds(STEPS * f, STEPS), :] = cols[j][c]


def merge_rows(src_ref, count, meet_ref):
    low = [src_ref[v, pl.ds(0, count, stride=2), :] for v in range(FORM)]
    high = [src_ref[v, pl.ds(1, count, stride=2), :] for v in range(FORM)]
    joined, meet = merge(low, high)
    for v in range(FORM):
        meet_ref[v] = meet[v]
    return joined


def merge_tree(form_ref, mid_ref, small_ref, meets):
    for v, item in enumerate(merge_rows(form_ref, 20, meets[0])):
        mid_ref[v] = item
    for v, item in enumerate(merge_rows(mid_ref, 10, meets[1])):
        small_ref[v] = item
    return merge_rows(small_ref, 5, meets[2])


def spread_tree(outside, meets, spreads):
    for meet_ref, out_ref, count in zip(meets[::-1], spreads, (5, 10, 20)):
        p0, p1, q0, q1 = (
            value_of([meet_ref[5 * x + c] for c in range(5)], outside) for x in range(4)
        )
        even = (outside[0], outside[1], p0, p1)
        odd = (q0, q1, outside[2], outside[3])
        for x in range(4):
            out_ref[x, pl.ds(0, count, stride=2), :] = even[x]
            out_ref[x, pl.ds(1, count, stride=2), :] = odd[x]
        outside = [out_ref[x] for x in range(4)]


def section_values(cols_ref, spread_ref, f, j):
    outside = [spread_ref[x, pl.ds(STEPS * f, STEPS), :] for x in range(4)]
    return value_of([cols_ref[c, f, j] for c in range(5)], outside)


def mix(matrix_ref, f, values):
    total = matrix_ref[f, 0] * values[0]
    for g in range(1, FIELDS):
        total = total + matrix_ref[f, g] * values[g]
    return total


def to_eta_rows(block):
    beside = pltpu.roll(block, LANES - 1, 1)
    return jnp.transpose(jnp.concatenate([block, beside], axis=0))


def from_eta_rows(rows):
    both = jnp.transpose(rows)
    half = both.shape[0] // 2
    lane = lax.broadcasted_iota(jnp.int32, (half, LANES), 1)
    return jnp.where(lane % 2 == 0, both[:half], pltpu.roll(both[half:], 1, 1))


def eta_reduce_kernel(
    residual_hbm, left_hbm, speed_hbm, damp_hbm,
    send_ref, cols_ref, meet0_ref, meet1_ref, meet2_ref,
    residual_ref, left_ref, speed_ref, damp_ref, sems,
    turned_ref, form_ref, mid_ref, small_ref,
):
    copies = [
        pltpu.make_async_copy(damp_hbm, damp_ref, sems.at[0]),
        pltpu.make_async_copy(speed_hbm, speed_ref, sems.at[1]),
        pltpu.make_async_copy(left_hbm, left_ref, sems.at[2]),
        pltpu.make_async_copy(residual_hbm, residual_ref, sems.at[3]),
    ]
    for copy in copies:
        copy.start()
    copies[0].wait()
    turned_ref[2 * FIELDS] = to_eta_rows(damp_ref[...])
    copies[1].wait()
    for f in range(FIELDS):
        turned_ref[FIELDS + f] = to_eta_rows(speed_ref[f])
    copies[2].wait()
    copies[3].wait()
    for f in range(FIELDS):
        turned_ref[f] = to_eta_rows(mix(left_ref, f, [residual_ref[g] for g in range(FIELDS)]))

    def cell(index, j):
        return turned_ref[index, pl.ds(SPAN * j, STEPS, stride=SPAN * STEPS), :]

    reduce_sections(
        cell,
        lambda f, j: cell(FIELDS + f, j),
        lambda j: cell(2 * FIELDS, j),
        cols_ref,
        form_ref,
    )
    block = merge_tree(form_ref, mid_ref, small_ref, (meet0_ref, meet1_ref, meet2_ref))
    for v in range(FORM):
        send_ref[pl.ds(FIELDS * v, FIELDS), :] = block[v]
    final = SPAN * (STEPS * STEPS - 1)
    for f in range(FIELDS):
        rims = (
            turned_ref[2 * FIELDS, pl.ds(0, 1), :],
            turned_ref[FIELDS + f, pl.ds(0, 1), :],
            turned_ref[2 * FIELDS, pl.ds(final, 1), :],
            turned_ref[FIELDS + f, pl.ds(final, 1), :],
        )
        for r in range(4):
            send_ref[pl.ds(FIELDS * (FORM + r) + f, 1), :] = rims[r]


def eta_outside(place_ref, got_ref, form_ref, mid_ref, small_ref, meets, spreads, all_ref, own_ref):
    row = section_rows()
    zero = jnp.zeros((STEPS, LANES), jnp.float32)
    rows_each = SENT * FIELDS
    pair_forms, pair_meets, rims = [], [], []
    for f in range(FIELDS):
        halves = [
            [
                got_ref[pl.ds(rows_each * side + FIELDS * v + f, STEPS, stride=2 * rows_each), :]
                for v in range(SENT)
            ]
            for side in range(2)
        ]
        even, odd = halves
        rim_even = (
            jnp.where(row == 0, zero, pltpu.roll(odd[22], 1, 0)),
            jnp.where(row == 0, zero, pltpu.roll(odd[23], 1, 0)),
            odd[20],
            odd[21],
        )
        rim_odd = (
            even[22],
            even[23],
            jnp.where(row == STEPS - 1, zero, pltpu.roll(even[20], STEPS - 1, 0)),
            jnp.where(row == STEPS - 1, zero, pltpu.roll(even[21], STEPS - 1, 0)),
        )
        low = plain_form(even[:FORM], *rim_even)
        high = plain_form(odd[:FORM], *rim_odd)
        joined, meet = merge(low, high)
        for v in range(FORM):
            form_ref[v, pl.ds(STEPS * f, STEPS), :] = joined[v]
        pair_meets.append(meet)
        pair_forms.append((low[:5], low[15:], high[:5], high[15:]))
        rims.append((rim_even, rim_odd))
    merge_tree(form_ref, mid_ref, small_ref, meets)
    nothing = jnp.zeros((FIELDS, LANES), jnp.float32)
    spread_tree([nothing] * 4, meets, spreads)
    place = place_ref[0]
    for f in range(FIELDS):
        l0, l1, r0, r1 = (spreads[2][x, pl.ds(STEPS * f, STEPS), :] for x in range(4))
        p0, p1, q0, q1 = (
            value_of(pair_meets[f][5 * x : 5 * x + 5], (l0, l1, r0, r1)) for x in range(4)
        )
        for side, around in enumerate(((l0, l1, p0, p1), (q0, q1, r0, r1))):
            first = value_of(pair_forms[f][2 * side], around)
            last = value_of(pair_forms[f][2 * side + 1], around)
            for x, item in enumerate(rim_terms(around, first, last, *rims[f][side])):
                all_ref[x, side, pl.ds(STEPS * f, STEPS), :] = item
        side = lax.rem(place, 2)
        pair = lax.div(place, 2)
        for x in range(4):
            own_ref[x, pl.ds(f, 1), :] = all_ref[x, side, pl.ds(STEPS * f + pair, 1), :]


def eta_finish_kernel(
    place_ref, got_ref, eta_cols_ref, eta_meet0_ref, eta_meet1_ref, eta_meet2_ref,
    middle_ref, speed_ref, damp_ref,
    send_ref, cols_ref, meet0_ref, meet1_ref, meet2_ref,
    form_ref, mid_ref, small_ref, spread0_ref, spread1_ref, spread2_ref, all_ref, own_ref,
    turned_ref, mixed_ref, square_ref,
):
    spreads = (spread0_ref, spread1_ref, spread2_ref)
    meets = (meet0_ref, meet1_ref, meet2_ref)
    eta_outside(place_ref, got_ref, form_ref, mid_ref, small_ref, meets, spreads, all_ref, own_ref)
    spread_tree(
        [own_ref[x] for x in range(4)], (eta_meet0_ref, eta_meet1_ref, eta_meet2_ref), spreads
    )
    solved = []
    for f in range(FIELDS):
        for j in range(STEPS):
            turned_ref[f, pl.ds(SPAN * j, STEPS, stride=SPAN * STEPS), :] = section_values(
                eta_cols_ref, spread2_ref, f, j
            )
        solved.append(from_eta_rows(turned_ref[f]))
    for f in range(FIELDS):
        mixed_ref[f] = mix(middle_ref, f, solved)
    reduce_sections(
        lambda f, j: mixed_ref[f, pl.ds(j, STEPS, stride=STEPS), :],
        lambda f, j: speed_ref[f, pl.ds(j, STEPS, stride=STEPS), :],
        lambda j: damp_ref[pl.ds(j, STEPS, stride=STEPS), :],
        cols_ref,
        form_ref,
    )
    block = merge_tree(form_ref, mid_ref, small_ref, meets)
    for v in range(FORM):
        square_ref[pl.ds(FIELDS * v, FIELDS), :] = block[v]
    final = STEPS * STEPS - 1
    for f in range(FIELDS):
        rims = (
            damp_ref[pl.ds(0, 1), :],
            speed_ref[f, pl.ds(0, 1), :],
            damp_ref[pl.ds(final, 1), :],
            speed_ref[f, pl.ds(final, 1), :],
        )
        for r in range(4):
            square_ref[pl.ds(FIELDS * (FORM + r) + f, 1), :] = rims[r]
    square_ref[pl.ds(SENT * FIELDS, LANES - SENT * FIELDS), :] = jnp.zeros(
        (LANES - SENT * FIELDS, LANES), jnp.float32
    )
    send_ref[...] = jnp.transpose(square_ref[...])


def xi_loop_kernel(got_ref, send_ref, square_ref):
    square_ref[...] = jnp.transpose(got_ref[...])
    items = [square_ref[pl.ds(FIELDS * v, FIELDS), :] for v in range(SENT)]
    width = 4

    def from_below(x, distance):
        return pltpu.roll(x, width * distance, 1)

    def from_above(x, distance):
        return pltpu.roll(x, LANES - width * distance, 1)

    rims = (
        from_below(items[22], 1),
        from_below(items[23], 1),
        from_above(items[20], 1),
        from_above(items[21], 1),
    )
    form = plain_form(items[:FORM], *rims)
    distance = 1
    while width * distance < LANES:
        form, unused = merge(form, [from_above(x, distance) for x in form])
        distance = 2 * distance
    rows = [form[5 * x : 5 * x + 5] for x in range(4)]
    e00, e01, e10, e11 = inverse_parts(
        1.0 + rows[0][3], rows[0][4], rows[1][3], 1.0 + rows[1][4]
    )
    first = [e11 * rows[0][c] - e01 * rows[1][c] for c in range(3)]
    second = [e00 * rows[1][c] - e10 * rows[0][c] for c in range(3)]
    left = [
        [row[c] - row[3] * first[c] - row[4] * second[c] for c in range(3)] for row in rows[2:]
    ]
    e00, e01, e10, e11 = inverse_parts(
        1.0 + left[0][1], left[0][2], left[1][1], 1.0 + left[1][2]
    )
    l0 = e11 * left[0][0] - e01 * left[1][0]
    l1 = e00 * left[1][0] - e10 * left[0][0]
    p0 = first[0] - first[1] * l0 - first[2] * l1
    p1 = second[0] - second[1] * l0 - second[2] * l1
    r0, r1 = from_above(p0, 1), from_above(p1, 1)
    terms = rim_terms([l0, l1, r0, r1], p0, from_above(l1, 1), *rims)
    square_ref[...] = jnp.zeros((LANES, LANES), jnp.float32)
    for x in range(4):
        square_ref[pl.ds(FIELDS * x, FIELDS), :] = terms[x]
    square_ref[...] = jnp.transpose(square_ref[...])
    devices = LANES // width
    total = square_ref[pl.ds(0, devices, stride=width), :]
    for part in range(1, width):
        piece = square_ref[pl.ds(part, devices, stride=width), :]
        total = total + pltpu.roll(piece, part * devices, 1)
    send_ref[...] = total


def xi_finish_kernel(
    got_ref, cols_ref, meet0_ref, meet1_ref, meet2_ref, right_ref,
    out_hbm,
    square_ref, spread0_ref, spread1_ref, spread2_ref, solved_ref, out_ref, sems,
):
    devices = got_ref.shape[0]
    width = LANES // devices
    got = got_ref[...]
    square_ref[pl.ds(0, devices, stride=width), :] = got
    for part in range(1, width):
        square_ref[pl.ds(part, devices, stride=width), :] = pltpu.roll(
            got, LANES - part * devices, 1
        )
    square_ref[...] = jnp.transpose(square_ref[...])
    outside = [square_ref[pl.ds(FIELDS * x, FIELDS), :] for x in range(4)]
    spread_tree(
        outside, (meet0_ref, meet1_ref, meet2_ref), (spread0_ref, spread1_ref, spread2_ref)
    )
    for f in range(FIELDS):
        for j in range(STEPS):
            solved_ref[f, pl.ds(j, STEPS, stride=STEPS), :] = section_values(
                cols_ref, spread2_ref, f, j
            )
    copies = []
    for f in range(FIELDS):
        out_ref[f] = mix(right_ref, f, [solved_ref[g] for g in range(FIELDS)])
        copies.append(pltpu.make_async_copy(out_ref.at[f], out_hbm.at[f], sems.at[f]))
        copies[f].start()
    for copy in copies:
        copy.wait()


def shape(*dims):
    return jax.ShapeDtypeStruct(dims, jnp.float32)


def vmem(*dims):
    return pltpu.VMEM(dims, jnp.float32)


KEPT = (
    shape(5, FIELDS, STEPS, STEPS, LANES),
    shape(FORM, 20, LANES),
    shape(FORM, 10, LANES),
    shape(FORM, 5, LANES),
)
FORMS = (vmem(FORM, 40, LANES), vmem(FORM, 20, LANES), vmem(FORM, 10, LANES))
SPREADS = (vmem(4, 10, LANES), vmem(4, 20, LANES), vmem(4, 40, LANES))


ON_CHIP = pl.BlockSpec(memory_space=pltpu.VMEM)
IN_PLACE = pl.BlockSpec(memory_space=pltpu.HBM)


def call(kernel, in_specs, outs, out_specs, scratch, name):
    return pl.pallas_call(
        kernel,
        out_shape=list(outs),
        in_specs=in_specs,
        out_specs=out_specs,
        scratch_shapes=list(scratch),
        compiler_params=pltpu.CompilerParams(vmem_limit_bytes=24 * 2**20),
        name=name,
    )


def in_place(*arrays):
    return [pltpu.with_memory_space_constraint(x, pltpu.HBM) for x in arrays]


def eta_reduce(residual, left_eta, speed_eta, damping_eta):
    fields, cells_xi, _ = residual.shape
    return call(
        eta_reduce_kernel,
        [IN_PLACE] * 4,
        (shape(SENT * FIELDS, LANES),) + KEPT,
        [ON_CHIP] * 5,
        (
            vmem(fields, cells_xi, LANES),
            vmem(fields, fields, cells_xi, LANES),
            vmem(fields, cells_xi, LANES),
            vmem(cells_xi, LANES),
            pltpu.SemaphoreType.DMA((4,)),
            vmem(2 * FIELDS + 1, LANES, LANES),
        )
        + FORMS,
        "eta_reduce",
    )(*in_place(residual, left_eta, speed_eta, damping_eta))


def eta_finish(place, eta_got, eta_kept, middle, speed_xi, damping_xi):
    cells_xi = damping_xi.shape[0]
    return call(
        eta_finish_kernel,
        [pl.BlockSpec(memory_space=pltpu.SMEM)] + [ON_CHIP] * 8,
        (shape(LANES, LANES),) + KEPT,
        [ON_CHIP] * 5,
        FORMS
        + SPREADS
        + (
            vmem(4, 2, 40, LANES),
            vmem(4, FIELDS, LANES),
            vmem(FIELDS, LANES, LANES),
            vmem(FIELDS, cells_xi, LANES),
            vmem(LANES, LANES),
        ),
        "eta_finish",
    )(place, eta_got, *eta_kept, middle, speed_xi, damping_xi)


def xi_loop(xi_got, loop):
    return call(
        xi_loop_kernel,
        [ON_CHIP],
        (shape(loop, LANES),),
        [ON_CHIP],
        (vmem(LANES, LANES),),
        "xi_loop",
    )(xi_got)[0]


def xi_finish(loop_got, xi_kept, right_xi):
    fields, _, cells_xi, cells_local = right_xi.shape
    return call(
        xi_finish_kernel,
        [ON_CHIP] * 6,
        (shape(fields, cells_xi, cells_local),),
        [IN_PLACE],
        (vmem(LANES, LANES),)
        + SPREADS
        + (
            vmem(FIELDS, cells_xi, LANES),
            vmem(FIELDS, cells_xi, LANES),
            pltpu.SemaphoreType.DMA((FIELDS,)),
        ),
        "xi_finish",
    )(loop_got, *xi_kept, right_xi)[0]


def per_device(residual, left_eta, middle, right_xi, speed_eta, speed_xi, damping_eta, damping_xi):
    eta_send, *eta_kept = eta_reduce(residual, left_eta, speed_eta, damping_eta)
    eta_got = lax.all_gather(eta_send, "eta", axis=0, tiled=True)
    place = lax.axis_index("eta").reshape(1).astype(jnp.int32)
    xi_send, *xi_kept = eta_finish(place, eta_got, eta_kept, middle, speed_xi, damping_xi)
    loop = lax.axis_size("xi")
    xi_got = lax.all_to_all(
        xi_send.reshape(loop, LANES // loop, LANES), "xi", 0, 0, tiled=True
    ).reshape(LANES, LANES)
    loop_got = lax.all_to_all(
        xi_loop(xi_got, loop).reshape(loop, 1, LANES), "xi", 0, 0, tiled=True
    ).reshape(loop, LANES)
    return xi_finish(loop_got, xi_kept, right_xi)


def solution(mesh):
    in_specs = (
        P(None, "xi", "eta"),
        P(None, None, "xi", "eta"),
        P(None, None, "xi", "eta"),
        P(None, None, "xi", "eta"),
        P(None, "xi", "eta"),
        P(None, "xi", "eta"),
        P("xi", "eta"),
        P("xi", "eta"),
    )
    out_specs = P(None, "xi", "eta")
    return jax.shard_map(
        per_device, mesh=mesh, in_specs=in_specs, out_specs=out_specs, check_vma=False
    )
```
